32 devices in a mesh: req: 8 (over z, x), tp: 4 (over y, core).
Axes of the slice: x: 2, y: 2, z: 4, core: 2. Of those that a mesh axis runs over, the one named last changes fastest.
Arguments:
- hidden_in: bfloat16 [1024, 4096], P(('req', 'tp')), may hold values from -6 to 6
- queries: bfloat16 [1024, 4096], P(('req', 'tp')), may hold values from -6 to 6
- new_keys: bfloat16 [1024, 1024], P(('req', 'tp')), may hold values from -6 to 6
- new_values: bfloat16 [1024, 1024], P(('req', 'tp')), may hold values from -6 to 6
- key_cache: bfloat16 [32768, 1024], P(('req', 'tp'))
- value_cache: bfloat16 [32768, 1024], P(('req', 'tp')), may hold values from -6 to 6
- cache_lengths: int32 [16], replicated, may hold values from 256 to 2048, as said below
- parent_ids: int32 [16, 64], replicated, may hold values from 0 to 62, as said below
- accepted_leaf: int32 [16], replicated, may hold values from 0 to 63
- query_gain: bfloat16 [128], replicated, may hold values from 0.5 to 1.5
- key_gain: bfloat16 [128], replicated, may hold values from 0.5 to 1.5
- post_gain: bfloat16 [4096], replicated, may hold values from 0.5 to 1.5
- out_weight: bfloat16 [4096, 4096], P('req', 'tp'), may hold values from -0.09375 to 0.09375
- gate_weight: bfloat16 [4096, 6144], P('req', 'tp'), may hold values from -0.09375 to 0.09375
- up_weight: bfloat16 [4096, 6144], P('req', 'tp'), may hold values from -0.09375 to 0.09375
- down_weight: bfloat16 [6144, 4096], P('tp', 'req'), may hold values from -0.078125 to 0.078125
Outputs:
- layer_out: bfloat16 [1024, 4096], P(('req', 'tp'))
- accepted_kv: bfloat16 [1024, 2048], P(('req', 'tp'))
The draws below stay inside these ranges and needn't reach their ends.
Inputs may be any that keep to these rules, and one draw needn't show every extreme that they name: `cache_lengths`: some request has exactly 2048 live positions and some exactly 256. parent_ids[r, 0] = 0; every other node j has a parent among nodes j - 4 to j - 1.
All inputs are finite; a program needn't handle non-finite values.
Results may differ from the reference program's by a relative error of at most 0.018.
Values may be sent and summed in bfloat16 or wider, within the bound.
A program may use at most 128 MiB of HBM per device.

```python
import jax
import jax.numpy as jnp
from jax import lax

D = 4096
HEADS = 32
KV_HEADS = 8
HEAD_DIM = 128
FF = 6144
TREE = 64
CAP = 2048
QDIM = 4096
KVDIM = 1024
REQ = 16
TOKENS = 1024
CACHE_ROWS = 32768


def draw_key_cache(key, part):
    drawn = jax.random.normal(jax.random.fold_in(key, 11), (CACHE_ROWS, KVDIM), jnp.float32)
    return drawn.astype(jnp.bfloat16)


def draw_cache_lengths(key, part):
    short_len = jax.random.randint(jax.random.fold_in(key, 21), (REQ,), CAP // 8, CAP // 4 + 1)
    long_len = jax.random.randint(jax.random.fold_in(key, 22), (REQ,), 3 * CAP // 4, CAP + 1)
    selector = jax.random.randint(jax.random.fold_in(key, 23), (REQ,), 0, 8)
    lengths = jnp.where(selector == 0, long_len, short_len)
    longest = jax.random.randint(jax.random.fold_in(key, 24), (), 0, REQ)
    lengths = lengths.at[longest].set(CAP)
    lengths = lengths.at[(longest + 1) % REQ].set(CAP // 8)
    return lengths.astype(jnp.int32)


def draw_parent_ids(key, part):
    node_ids = jnp.arange(TREE, dtype=jnp.int32)
    step_back = jax.random.randint(jax.random.fold_in(key, 31), (REQ, TREE), 0, 4)
    step_back = jnp.minimum(step_back, jnp.maximum(node_ids - 1, 0)[None, :])
    return jnp.where(node_ids[None, :] == 0, 0, node_ids[None, :] - 1 - step_back).astype(jnp.int32)


def plant(values, own_key, low, high):
    longest = values.shape.index(max(values.shape))
    spots = []
    for shift in (0, 1):
        where = [jax.random.randint(jax.random.fold_in(own_key, axis), (), 0, length) for axis, length in enumerate(values.shape)]
        where[longest] = (where[longest] + shift) % values.shape[longest]
        spots.append(tuple(where))
    return values.at[spots[0]].set(low).at[spots[1]].set(high)


def level_of(rng, shape, shards, least, high):
    factor_of = 1.0
    for axis_at, blocks in shards:
        draws = jax.random.uniform(jax.random.fold_in(jax.random.fold_in(rng, 6), axis_at), (blocks,), jnp.float32, least / len(shards), high / len(shards))
        factor_of = factor_of * jnp.repeat(jnp.exp(draws), shape[axis_at] // blocks).reshape((-1,) + (1,) * (len(shape) - 1 - axis_at))
    return factor_of


def noise(key, shape, spread, most, split=(), kind=jnp.bfloat16):
    entries = spread * jax.random.normal(key, shape, jnp.float32)
    if split:
        entries = entries * level_of(key, shape, split, -0.22, 0.18)
    return jnp.clip(entries, -most, most).astype(kind)


def setup_inputs(seed: int = 0) -> dict:
    key_of = jax.random.split(jax.random.key(seed), 17)
    return {
        "hidden_in": noise(key_of[0], (TOKENS, D), 1.0, 6.0, ((0, 32),)),
        "queries": noise(key_of[1], (TOKENS, QDIM), 1.0, 6.0, ((0, 32),)),
        "new_keys": noise(key_of[2], (TOKENS, KVDIM), 1.0, 6.0, ((0, 32),)),
        "new_values": noise(key_of[3], (TOKENS, KVDIM), 1.0, 6.0, ((0, 32),)),
        "key_cache": draw_key_cache(jax.random.fold_in(key_of[16], 71), 0),
        "value_cache": noise(key_of[5], (CACHE_ROWS, KVDIM), 1.0, 6.0, ((0, 32),)),
        "cache_lengths": draw_cache_lengths(jax.random.fold_in(key_of[16], 71), 0),
        "parent_ids": draw_parent_ids(jax.random.fold_in(key_of[16], 71), 0),
        "accepted_leaf": plant(jax.random.randint(key_of[8], (REQ,), 0, TREE), jax.random.fold_in(key_of[8], 1), 0, TREE - 1).astype(jnp.int32),
        "query_gain": jnp.clip(1.0 + 0.1 * jax.random.normal(key_of[9], (HEAD_DIM,), jnp.float32), 0.5, 1.5).astype(jnp.bfloat16),
        "key_gain": jnp.clip(1.0 + 0.1 * jax.random.normal(key_of[10], (HEAD_DIM,), jnp.float32), 0.5, 1.5).astype(jnp.bfloat16),
        "post_gain": jnp.clip(1.0 + 0.1 * jax.random.normal(key_of[11], (D,), jnp.float32), 0.5, 1.5).astype(jnp.bfloat16),
        "out_weight": noise(key_of[12], (QDIM, D), QDIM ** -0.5, 0.09375, ((0, 8), (1, 4))),
        "gate_weight": noise(key_of[13], (D, FF), D ** -0.5, 0.09375, ((0, 8), (1, 4))),
        "up_weight": noise(key_of[14], (D, FF), D ** -0.5, 0.09375, ((0, 8), (1, 4))),
        "down_weight": noise(key_of[15], (FF, D), FF ** -0.5, 0.078125, ((0, 4), (1, 8))),
    }


NEG = -1e+30
EPS = 1e-06
ROPE_BASE = 1000000.0

def settle(values):
    return lax.optimization_barrier(values.astype(jnp.bfloat16)).astype(jnp.float32)

def head_norm(values, gain_vec):
    mean_sq = lax.optimization_barrier(jnp.mean(values * values, axis=-1, keepdims=True))
    return values * lax.rsqrt(mean_sq + EPS) * gain_vec.astype(jnp.float32)

def rotate(values, position):
    head_width = values.shape[-1]
    half_width = head_width // 2
    frequency = ROPE_BASE ** (-2.0 * jnp.arange(half_width, dtype=jnp.float32) / head_width)
    angles = position[:, None] * frequency[None, :]
    cosine = jnp.cos(angles)[:, None, :]
    sine_part = jnp.sin(angles)[:, None, :]
    front_half = values[..., :half_width]
    back_half = values[..., half_width:]
    return jnp.concatenate([front_half * cosine - back_half * sine_part, back_half * cosine + front_half * sine_part], axis=-1)

def ancestors(parent_row):
    node_count = parent_row.shape[0]
    node_ids = jnp.arange(node_count, dtype=jnp.int32)
    identity_mat = (node_ids[:, None] == node_ids[None, :]).astype(jnp.float32)
    parent_mat = (parent_row[:, None] == node_ids[None, :]).astype(jnp.float32) * (1.0 - identity_mat)
    reached = jnp.minimum(identity_mat + parent_mat, 1.0)
    for sweep in range(node_count.bit_length()):
        reached = jnp.minimum(jnp.dot(reached, reached, precision=lax.Precision.HIGHEST), 1.0)
    return reached

def reference(hidden_in, queries, new_keys, new_values, key_cache, value_cache, cache_lengths, parent_ids, accepted_leaf, query_gain, key_gain, post_gain, out_weight, gate_weight, up_weight, down_weight):
    group_size = HEADS // KV_HEADS
    score_scale = HEAD_DIM ** (-0.5)

    def one_request(packed):
        query_rows, key_rows, value_rows, cache_keys, cache_values, cache_length, parent_row, leaf_index = packed
        reached = ancestors(parent_row)
        node_depth = lax.optimization_barrier(jnp.sum(reached, axis=1)) - 1.0
        position = cache_length.astype(jnp.float32) + node_depth
        query_heads = rotate(head_norm(query_rows.astype(jnp.float32).reshape(TREE, HEADS, HEAD_DIM), query_gain), position).astype(jnp.bfloat16)
        key_heads = rotate(head_norm(key_rows.astype(jnp.float32).reshape(TREE, KV_HEADS, HEAD_DIM), key_gain), position).astype(jnp.bfloat16)
        grouped = query_heads.astype(jnp.float32).reshape(TREE, KV_HEADS, group_size, HEAD_DIM)
        stored_keys = cache_keys.astype(jnp.float32).reshape(CAP, KV_HEADS, HEAD_DIM)
        stored_values = cache_values.astype(jnp.float32).reshape(CAP, KV_HEADS, HEAD_DIM)
        draft_values = value_rows.astype(jnp.float32).reshape(TREE, KV_HEADS, HEAD_DIM)
        live_slots = jnp.arange(CAP, dtype=jnp.int32) < cache_length
        tree_mask = reached > 0.5
        cache_scores = jnp.where(live_slots, jnp.einsum('qhgd,khd->hgqk', grouped, stored_keys) * score_scale, NEG)
        tree_scores = jnp.where(tree_mask, jnp.einsum('qhgd,khd->hgqk', grouped, key_heads.astype(jnp.float32)) * score_scale, NEG)
        row_top = jnp.maximum(lax.optimization_barrier(jnp.max(cache_scores, axis=-1, keepdims=True)), lax.optimization_barrier(jnp.max(tree_scores, axis=-1, keepdims=True)))
        cache_weights = settle(jnp.where(live_slots, jnp.exp(cache_scores - row_top), 0.0))
        tree_weights = settle(jnp.where(tree_mask, jnp.exp(tree_scores - row_top), 0.0))
        weight_total = lax.optimization_barrier(jnp.sum(cache_weights, axis=-1, keepdims=True)) + lax.optimization_barrier(jnp.sum(tree_weights, axis=-1, keepdims=True))
        mixed = jnp.einsum('hgqk,khd->hgqd', cache_weights, stored_values) + jnp.einsum('hgqk,khd->hgqd', tree_weights, draft_values)
        attended = jnp.transpose(mixed / weight_total, (2, 0, 1, 3)).reshape(TREE, QDIM).astype(jnp.bfloat16)
        node_ids = jnp.arange(TREE, dtype=jnp.int32)
        leaf_pick = (node_ids == leaf_index).astype(jnp.float32)
        leaf_row = jnp.dot(leaf_pick, reached, precision=lax.Precision.HIGHEST)
        chosen = leaf_row[None, :] * (node_depth[None, :] == node_ids[:, None].astype(jnp.float32)).astype(jnp.float32)
        fresh_rows = jnp.concatenate([key_heads.reshape(TREE, KVDIM), value_rows], axis=1)
        compact = jnp.dot(chosen.astype(jnp.bfloat16), fresh_rows, preferred_element_type=jnp.float32).astype(jnp.bfloat16)
        return (attended, compact)
    attended, compact = lax.map(one_request, (queries.reshape(REQ, TREE, QDIM), new_keys.reshape(REQ, TREE, KVDIM), new_values.reshape(REQ, TREE, KVDIM), key_cache.reshape(REQ, CAP, KVDIM), value_cache.reshape(REQ, CAP, KVDIM), cache_lengths, parent_ids, accepted_leaf))
    attended = attended.reshape(TOKENS, QDIM)
    projected = jnp.dot(attended, out_weight, preferred_element_type=jnp.float32)
    residual = settle(hidden_in.astype(jnp.float32) + projected)
    mean_sq = lax.optimization_barrier(jnp.mean(residual * residual, axis=-1, keepdims=True))
    normed = (residual * lax.rsqrt(mean_sq + EPS) * post_gain.astype(jnp.float32)).astype(jnp.bfloat16)
    gate_sum = jnp.dot(normed, gate_weight, preferred_element_type=jnp.float32)
    up_sum = jnp.dot(normed, up_weight, preferred_element_type=jnp.float32)
    hidden = (jax.nn.silu(gate_sum) * up_sum).astype(jnp.bfloat16)
    mlp_sum = jnp.dot(hidden, down_weight, preferred_element_type=jnp.float32)
    layer_out = (residual + mlp_sum).astype(jnp.bfloat16)
    return (layer_out, compact.reshape(TOKENS, 2 * KVDIM))
```

```python
import jax
import jax.numpy as jnp
from jax import lax
from jax.sharding import PartitionSpec as P

HEADS = 32
KV_HEADS = 8
HEAD_DIM = 128


NEG = -1e30
EPS = 1e-06
ROPE_BASE = 1000000.0


def swapped(value, axis, bit):
    mask = 2**bit
    pairs = [(source, source ^ mask) for source in range(lax.axis_size(axis))]
    return lax.ppermute(value, axis, pairs)


def head_norm(values, gain_vec):
    mean_sq = jnp.mean(values * values, axis=-1, keepdims=True)
    return values * lax.rsqrt(mean_sq + EPS) * gain_vec.astype(jnp.float32)


def rotate(values, position):
    head_width = values.shape[-1]
    half_width = head_width // 2
    frequency = ROPE_BASE ** (-2.0 * jnp.arange(half_width, dtype=jnp.float32) / head_width)
    angles = position[:, None] * frequency[None, :]
    cosine = jnp.cos(angles)[:, None, :]
    sine_part = jnp.sin(angles)[:, None, :]
    front_half = values[..., :half_width]
    back_half = values[..., half_width:]
    return jnp.concatenate(
        [front_half * cosine - back_half * sine_part, back_half * cosine + front_half * sine_part],
        axis=-1,
    )


def ancestors(parent_row):
    node_count = parent_row.shape[0]
    node_ids = jnp.arange(node_count, dtype=jnp.int32)
    identity_mat = (node_ids[:, None] == node_ids[None, :]).astype(jnp.float32)
    parent_mat = (parent_row[:, None] == node_ids[None, :]).astype(jnp.float32) * (
        1.0 - identity_mat
    )
    reached = jnp.minimum(identity_mat + parent_mat, 1.0)
    for sweep in range(node_count.bit_length()):
        reached = jnp.minimum(jnp.dot(reached, reached, precision=lax.Precision.HIGHEST), 1.0)
    return reached


def per_device(
    hidden_in,
    queries,
    new_keys,
    new_values,
    key_cache,
    value_cache,
    cache_lengths,
    parent_ids,
    accepted_leaf,
    query_gain,
    key_gain,
    post_gain,
    out_weight,
    gate_weight,
    up_weight,
    down_weight,
):
    half_rows = queries.shape[0]
    tree_size = 2 * half_rows
    group_size = HEADS // KV_HEADS
    kv_width = new_keys.shape[1]
    q_width = queries.shape[1]
    score_scale = HEAD_DIM ** (-0.5)
    tp_count = lax.axis_size("tp")
    device = lax.axis_index(("req", "tp"))
    request = device // 2
    pair_side = lax.axis_index("tp") % 2
    cache_length = lax.dynamic_index_in_dim(cache_lengths, request, 0, keepdims=False)
    parent_row = lax.dynamic_index_in_dim(parent_ids, request, 0, keepdims=False)
    leaf_index = lax.dynamic_index_in_dim(accepted_leaf, request, 0, keepdims=False)
    reached = ancestors(parent_row)
    node_depth = jnp.sum(reached, axis=1) - 1.0
    node_ids = jnp.arange(tree_size, dtype=jnp.int32)
    local_ids = jnp.arange(half_rows, dtype=jnp.int32)
    node_order = jnp.concatenate(
        [pair_side * half_rows + local_ids, (1 - pair_side) * half_rows + local_ids]
    )
    reorder = (node_order[:, None] == node_ids[None, :]).astype(jnp.float32)
    reached_rows = jnp.dot(reorder, reached, precision=lax.Precision.HIGHEST)
    own_cols = jnp.dot(reached_rows, reorder[:half_rows].T, precision=lax.Precision.HIGHEST) > 0.5
    own_depth = jnp.dot(reorder[:half_rows], node_depth, precision=lax.Precision.HIGHEST)
    position = cache_length.astype(jnp.float32) + own_depth
    query_heads = rotate(
        head_norm(queries.astype(jnp.float32).reshape(half_rows, HEADS, HEAD_DIM), query_gain),
        position,
    ).astype(jnp.bfloat16)
    key_heads = rotate(
        head_norm(new_keys.astype(jnp.float32).reshape(half_rows, KV_HEADS, HEAD_DIM), key_gain),
        position,
    ).astype(jnp.bfloat16)
    query_own = query_heads.reshape(half_rows, q_width)
    fresh_own = jnp.concatenate([key_heads.reshape(half_rows, kv_width), new_values], axis=1)
    query_other, fresh_other = swapped((query_own, fresh_own), "tp", 0)
    query_all = jnp.concatenate([query_own, query_other], axis=0).reshape(
        tree_size, KV_HEADS, group_size, HEAD_DIM
    )

    def attend(running, block_keys, block_values, allowed):
        run_top, run_total, summed = running
        scores = (
            jnp.einsum("qhgd,khd->hgqk", query_all, block_keys, preferred_element_type=jnp.float32)
            * score_scale
        )
        scores = jnp.where(allowed, scores, NEG)
        new_top = jnp.maximum(run_top, jnp.max(scores, axis=-1, keepdims=True))
        weights = jnp.where(allowed, jnp.exp(scores - new_top), 0.0).astype(jnp.bfloat16)
        shrink = jnp.exp(run_top - new_top)
        run_total = run_total * shrink + jnp.sum(
            weights.astype(jnp.float32), axis=-1, keepdims=True
        )
        summed = summed * shrink + jnp.einsum(
            "hgqk,khd->hgqd", weights, block_values, preferred_element_type=jnp.float32
        )
        return (new_top, run_total, summed)

    shard_rows = key_cache.shape[0]
    block_rows = shard_rows // 8
    key_blocks = key_cache.reshape(8, block_rows, KV_HEADS, HEAD_DIM)
    value_blocks = value_cache.reshape(8, block_rows, KV_HEADS, HEAD_DIM)
    first_block = pair_side * 8
    stride = 1
    needed = (cache_length + block_rows - 1) // block_rows
    live_blocks = jnp.clip((needed - first_block + stride - 1) // stride, 0, 8)

    def cache_step(block_index, running):
        block_keys = lax.dynamic_index_in_dim(key_blocks, block_index, 0, keepdims=False)
        block_values = lax.dynamic_index_in_dim(value_blocks, block_index, 0, keepdims=False)
        first_slot = (first_block + stride * block_index) * block_rows
        allowed = first_slot + jnp.arange(block_rows, dtype=jnp.int32) < cache_length
        allowed = jnp.broadcast_to(allowed[None, :], (tree_size, block_rows))
        return attend(running, block_keys, block_values, allowed)

    initial = (
        jnp.full((KV_HEADS, group_size, tree_size, 1), NEG, jnp.float32),
        jnp.zeros((KV_HEADS, group_size, tree_size, 1), jnp.float32),
        jnp.zeros((KV_HEADS, group_size, tree_size, HEAD_DIM), jnp.float32),
    )
    running = lax.fori_loop(0, live_blocks, cache_step, initial)
    running = attend(
        running, key_heads, new_values.reshape(half_rows, KV_HEADS, HEAD_DIM), own_cols
    )
    run_top, run_total, summed = running
    far_top, far_total, far_sum = (
        swapped(run_top[:, :, half_rows:].astype(jnp.bfloat16), "tp", 0).astype(jnp.float32),
        swapped(run_total[:, :, half_rows:].astype(jnp.bfloat16), "tp", 0).astype(jnp.float32),
        swapped(summed[:, :, half_rows:].astype(jnp.bfloat16), "tp", 0).astype(jnp.float32),
    )
    near_top = run_top[:, :, :half_rows]
    joint_top = jnp.maximum(near_top, far_top)
    near_scale = jnp.exp(near_top - joint_top)
    far_scale = jnp.exp(far_top - joint_top)
    denominator = run_total[:, :, :half_rows] * near_scale + far_total * far_scale
    merged = (summed[:, :, :half_rows] * near_scale + far_sum * far_scale) / denominator
    attended = jnp.transpose(merged, (2, 0, 1, 3)).reshape(half_rows, q_width).astype(jnp.bfloat16)
    leaf_pick = (node_ids == leaf_index).astype(jnp.float32)
    leaf_row = jnp.dot(leaf_pick, reached, precision=lax.Precision.HIGHEST)
    out_depths = (pair_side * half_rows + local_ids).astype(jnp.float32)
    chosen = leaf_row[None, :] * (node_depth[None, :] == out_depths[:, None]).astype(jnp.float32)
    chosen = jnp.dot(chosen, reorder.T, precision=lax.Precision.HIGHEST)
    fresh_all = jnp.concatenate([fresh_own, fresh_other], axis=0)
    accepted_kv = jnp.dot(
        chosen.astype(jnp.bfloat16), fresh_all, preferred_element_type=jnp.float32
    ).astype(jnp.bfloat16)
    req_count = lax.axis_size("req")

    def feature_slices(rows):
        parts = rows.reshape(half_rows, req_count, -1)
        parts = jnp.transpose(parts, (1, 0, 2))
        parts = lax.all_to_all(parts, "req", split_axis=0, concat_axis=0, tiled=True)
        parts = lax.all_gather(parts[:, None], "tp", axis=1, tiled=True)
        return parts.reshape(req_count * tp_count * half_rows, -1)

    attn_slice = feature_slices(attended)
    projected = jnp.dot(attn_slice, out_weight, preferred_element_type=jnp.float32)
    projected = lax.psum_scatter(
        projected.astype(jnp.bfloat16), "req", scatter_dimension=0, tiled=True
    )
    own_projected = lax.all_to_all(
        projected, "tp", split_axis=0, concat_axis=1, tiled=True
    ).astype(jnp.float32)
    residual = (hidden_in.astype(jnp.float32) + own_projected).astype(jnp.bfloat16)
    residual_wide = residual.astype(jnp.float32)
    mean_sq = jnp.mean(residual_wide * residual_wide, axis=-1, keepdims=True)
    normed = (residual_wide * lax.rsqrt(mean_sq + EPS) * post_gain.astype(jnp.float32)).astype(
        jnp.bfloat16
    )
    normed_slice = feature_slices(normed)
    gate_part = jnp.dot(normed_slice, gate_weight, preferred_element_type=jnp.float32)
    up_part = jnp.dot(normed_slice, up_weight, preferred_element_type=jnp.float32)
    gate_sum = lax.psum_scatter(
        gate_part.astype(jnp.bfloat16), "req", scatter_dimension=0, tiled=True
    ).astype(jnp.float32)
    up_sum = lax.psum_scatter(
        up_part.astype(jnp.bfloat16), "req", scatter_dimension=0, tiled=True
    ).astype(jnp.float32)
    hidden = (jax.nn.silu(gate_sum) * up_sum).astype(jnp.bfloat16)
    hidden_all = lax.all_gather(hidden, "req", axis=0, tiled=True)
    partial_out = jnp.dot(hidden_all, down_weight, preferred_element_type=jnp.float32)
    partial_out = partial_out.astype(jnp.bfloat16).reshape(req_count, tp_count, half_rows, -1)
    partial_out = jnp.transpose(partial_out, (1, 0, 2, 3)).reshape(
        tp_count * req_count * half_rows, -1
    )
    paired_sum = lax.psum_scatter(partial_out, "tp", scatter_dimension=0, tiled=True)
    mlp_own = lax.all_to_all(
        paired_sum, "req", split_axis=0, concat_axis=1, tiled=True
    ).astype(jnp.float32)
    layer_out = (residual_wide + mlp_own).astype(jnp.bfloat16)
    return (layer_out, accepted_kv)


def solution(mesh):
    in_specs = (
        P(("req", "tp"), None),
        P(("req", "tp"), None),
        P(("req", "tp"), None),
        P(("req", "tp"), None),
        P(("req", "tp"), None),
        P(("req", "tp"), None),
        P(),
        P(),
        P(),
        P(),
        P(),
        P(),
        P("req", "tp"),
        P("req", "tp"),
        P("req", "tp"),
        P("tp", "req"),
    )
    out_specs = (P(("req", "tp"), None), P(("req", "tp"), None))
    return jax.shard_map(
        per_device, mesh=mesh, in_specs=in_specs, out_specs=out_specs, check_vma=False
    )
```

```python
import functools

import jax
import jax.numpy as jnp
from jax import lax
from jax.experimental import pallas as pl
from jax.experimental.pallas import tpu as pltpu
from jax.sharding import PartitionSpec as P

HEADS = 32
KV_HEADS = 8
HEAD_DIM = 128


NEG = -1e30
EPS = 1e-06
ROPE_BASE = 1000000.0


def swapped(value, axis, bit):
    mask = 2**bit
    pairs = [(source, source ^ mask) for source in range(lax.axis_size(axis))]
    return lax.ppermute(value, axis, pairs)


def head_norm(values, gain_vec):
    mean_sq = jnp.mean(values * values, axis=-1, keepdims=True)
    return values * lax.rsqrt(mean_sq + EPS) * gain_vec.astype(jnp.float32)


def rotate(values, position):
    head_width = values.shape[-1]
    half_width = head_width // 2
    frequency = ROPE_BASE ** (-2.0 * jnp.arange(half_width, dtype=jnp.float32) / head_width)
    angles = position[:, None] * frequency[None, :]
    cosine = jnp.cos(angles)[:, None, :]
    sine_part = jnp.sin(angles)[:, None, :]
    front_half = values[..., :half_width]
    back_half = values[..., half_width:]
    return jnp.concatenate(
        [front_half * cosine - back_half * sine_part, back_half * cosine + front_half * sine_part],
        axis=-1,
    )


SIDE = 2
MESH = pl.DeviceIdType.MESH
ANY = pl.BlockSpec(memory_space=pl.ANY)


def meet(peers):
    barrier = pltpu.get_barrier_semaphore()
    for peer in peers:
        pl.semaphore_signal(barrier, inc=1, device_id=peer, device_id_type=MESH)
    pl.semaphore_wait(barrier, len(peers))


def remote(source, target, send_sem, recv_sem, peer):
    return pltpu.make_async_remote_copy(
        src_ref=source,
        dst_ref=target,
        send_sem=send_sem,
        recv_sem=recv_sem,
        device_id=peer,
        device_id_type=MESH,
    )


def exchange_kernel(along, mode, rows_ref, out_ref, send_sem, recv_sem, own_sem):
    tp_count = lax.axis_size("tp")
    req, tp = lax.axis_index("req"), lax.axis_index("tp")
    level, side = req // SIDE, req % SIDE
    if along == "level":
        count, mine = lax.axis_size("req") // SIDE, level
    else:
        count, mine = SIDE * tp_count, side * tp_count + tp

    def device(index):
        if along == "level":
            return {"req": index * SIDE + side, "tp": tp}
        return {"req": level * SIDE + index // tp_count, "tp": index % tp_count}

    def part(index):
        if mode == "copy":
            return rows_ref
        if mode == "inner":
            return rows_ref.at[:, index]
        return rows_ref.at[index]

    others = [(mine + step) % count for step in range(1, count)]
    meet([device(index) for index in others])
    copies = [
        remote(part(index), out_ref.at[mine], send_sem.at[at], recv_sem.at[at], device(index))
        for at, index in enumerate(others)
    ]
    for copy in copies:
        copy.start()
    own = pltpu.make_async_copy(part(mine), out_ref.at[mine], own_sem)
    own.start()
    for copy in copies:
        copy.wait()
    own.wait()


def exchange(rows, along, mode, collective_id):
    count = lax.axis_size("req") // SIDE if along == "level" else SIDE * lax.axis_size("tp")
    if mode == "copy":
        part_shape = rows.shape
    elif mode == "inner":
        part_shape = rows.shape[:1] + rows.shape[2:]
    else:
        part_shape = rows.shape[1:]
    return pl.pallas_call(
        functools.partial(exchange_kernel, along, mode),
        out_shape=jax.ShapeDtypeStruct((count, *part_shape), rows.dtype),
        in_specs=[ANY],
        out_specs=ANY,
        scratch_shapes=[
            pltpu.SemaphoreType.DMA((count - 1,)),
            pltpu.SemaphoreType.DMA((count - 1,)),
            pltpu.SemaphoreType.DMA,
        ],
        compiler_params=pltpu.CompilerParams(collective_id=collective_id, has_side_effects=True),
    )(rows)


def slices_kernel(
    rows_ref, out_ref, send_level, recv_level, send_far, recv_far, send_core, recv_core, own_sem
):
    tp_count = lax.axis_size("tp")
    levels = lax.axis_size("req") // SIDE
    req, tp = lax.axis_index("req"), lax.axis_index("tp")
    level, side = req // SIDE, req % SIDE
    place = side * tp_count + tp
    core, chip = tp % 2, place // 2
    chips = SIDE * tp_count // 2
    width = rows_ref.shape[1] // levels

    def columns(index):
        return rows_ref.at[:, pl.ds(pl.multiple_of(index * width, width), width)]

    def chip_place(index):
        return index * 2 + core

    def device(at):
        return {"req": level * SIDE + at // tp_count, "tp": at % tp_count}

    level_ids = [(level + step) % levels for step in range(1, levels)]
    level_devices = [{"req": index * SIDE + side, "tp": tp} for index in level_ids]
    far_devices = [device(chip_place((chip + step) % chips)) for step in range(1, chips)]
    core_device = device(chip * 2 + 1 - core)
    meet(level_devices + far_devices + [core_device])
    first = [
        remote(columns(index), out_ref.at[level, place], send_level.at[at], recv_level.at[at], peer)
        for at, (index, peer) in enumerate(zip(level_ids, level_devices))
    ]
    for copy in first:
        copy.start()
    own = pltpu.make_async_copy(columns(level), out_ref.at[level, place], own_sem)
    own.start()
    for copy in first:
        copy.wait()
    own.wait()
    mine = out_ref.at[:, place]
    far = [
        remote(mine, mine, send_far.at[at], recv_far.at[at], peer)
        for at, peer in enumerate(far_devices)
    ]
    for copy in far:
        copy.start()
    near = [remote(mine, mine, send_core.at[0], recv_core.at[0], core_device)]
    near[0].start()
    for step in range(1, chips):
        far[step - 1].wait_recv()
        landed = out_ref.at[:, chip_place((chip - step + chips) % chips)]
        copy = remote(landed, landed, send_core.at[step], recv_core.at[step], core_device)
        copy.start()
        near.append(copy)
    for copy in near:
        copy.wait()
    for copy in far:
        copy.wait_send()


def feature_slices(rows, collective_id):
    levels = lax.axis_size("req") // SIDE
    places = SIDE * lax.axis_size("tp")
    width = rows.shape[1] // levels
    chips = places // 2
    gathered = pl.pallas_call(
        slices_kernel,
        out_shape=jax.ShapeDtypeStruct((levels, places, rows.shape[0], width), rows.dtype),
        in_specs=[ANY],
        out_specs=ANY,
        scratch_shapes=[
            pltpu.SemaphoreType.DMA((levels - 1,)),
            pltpu.SemaphoreType.DMA((levels - 1,)),
            pltpu.SemaphoreType.DMA((chips - 1,)),
            pltpu.SemaphoreType.DMA((chips - 1,)),
            pltpu.SemaphoreType.DMA((chips,)),
            pltpu.SemaphoreType.DMA((chips,)),
            pltpu.SemaphoreType.DMA,
        ],
        compiler_params=pltpu.CompilerParams(collective_id=collective_id, has_side_effects=True),
    )(rows)
    return gathered.reshape(-1, width)


def paired_halves(shard, axis):
    side = lax.axis_index("req") % SIDE
    half = shard.shape[axis] // 2
    kept = lax.dynamic_slice_in_dim(shard, side * half, half, axis)
    sent = lax.dynamic_slice_in_dim(shard, (1 - side) * half, half, axis)
    return kept, sent


def joined(kept, received, axis):
    side = lax.axis_index("req") % SIDE
    low = jnp.where(side == 0, kept, received)
    high = jnp.where(side == 0, received, kept)
    return jnp.concatenate([low, high], axis=axis)


def ancestors(parent_row):
    node_count = parent_row.shape[0]
    node_ids = jnp.arange(node_count, dtype=jnp.int32)
    identity_mat = (node_ids[:, None] == node_ids[None, :]).astype(jnp.float32)
    parent_mat = (parent_row[:, None] == node_ids[None, :]).astype(jnp.float32) * (
        1.0 - identity_mat
    )
    reached = jnp.minimum(identity_mat + parent_mat, 1.0)
    for sweep in range(node_count.bit_length()):
        reached = jnp.minimum(jnp.dot(reached, reached, precision=lax.Precision.HIGHEST), 1.0)
    return reached


def per_device(
    hidden_in,
    queries,
    new_keys,
    new_values,
    key_cache,
    value_cache,
    cache_lengths,
    parent_ids,
    accepted_leaf,
    query_gain,
    key_gain,
    post_gain,
    out_weight,
    gate_weight,
    up_weight,
    down_weight,
):
    half_rows = queries.shape[0]
    out_kept, out_sent = paired_halves(out_weight, 1)
    out_received = swapped(out_sent, "req", 0)
    gate_kept, gate_sent = paired_halves(gate_weight, 1)
    up_kept, up_sent = paired_halves(up_weight, 1)
    gate_up_received = swapped(jnp.concatenate([gate_sent, up_sent], axis=1), "req", 0)
    gate_up_kept = jnp.concatenate([gate_kept, up_kept], axis=1)
    down_kept, down_sent = paired_halves(down_weight, 0)
    down_received = swapped(down_sent, "req", 0)
    out_full = joined(out_kept, out_received, 0)
    gate_up_full = joined(gate_up_kept, gate_up_received, 0)
    down_full = joined(down_kept, down_received, 1)
    tree_size = 2 * half_rows
    group_size = HEADS // KV_HEADS
    kv_width = new_keys.shape[1]
    q_width = queries.shape[1]
    score_scale = HEAD_DIM ** (-0.5)
    tp_count = lax.axis_size("tp")
    device = lax.axis_index(("req", "tp"))
    request = device // 2
    pair_side = lax.axis_index("tp") % 2
    cache_length = lax.dynamic_index_in_dim(cache_lengths, request, 0, keepdims=False)
    parent_row = lax.dynamic_index_in_dim(parent_ids, request, 0, keepdims=False)
    leaf_index = lax.dynamic_index_in_dim(accepted_leaf, request, 0, keepdims=False)
    reached = ancestors(parent_row)
    node_depth = jnp.sum(reached, axis=1) - 1.0
    node_ids = jnp.arange(tree_size, dtype=jnp.int32)
    local_ids = jnp.arange(half_rows, dtype=jnp.int32)
    node_order = jnp.concatenate(
        [pair_side * half_rows + local_ids, (1 - pair_side) * half_rows + local_ids]
    )
    reorder = (node_order[:, None] == node_ids[None, :]).astype(jnp.float32)
    reached_rows = jnp.dot(reorder, reached, precision=lax.Precision.HIGHEST)
    own_cols = jnp.dot(reached_rows, reorder[:half_rows].T, precision=lax.Precision.HIGHEST) > 0.5
    own_depth = jnp.dot(reorder[:half_rows], node_depth, precision=lax.Precision.HIGHEST)
    position = cache_length.astype(jnp.float32) + own_depth
    query_heads = rotate(
        head_norm(queries.astype(jnp.float32).reshape(half_rows, HEADS, HEAD_DIM), query_gain),
        position,
    ).astype(jnp.bfloat16)
    key_heads = rotate(
        head_norm(new_keys.astype(jnp.float32).reshape(half_rows, KV_HEADS, HEAD_DIM), key_gain),
        position,
    ).astype(jnp.bfloat16)
    query_own = query_heads.reshape(half_rows, q_width)
    fresh_own = jnp.concatenate([key_heads.reshape(half_rows, kv_width), new_values], axis=1)
    query_other, fresh_other = swapped((query_own, fresh_own), "tp", 0)
    query_all = jnp.concatenate([query_own, query_other], axis=0).reshape(
        tree_size, KV_HEADS, group_size, HEAD_DIM
    )

    def attend(running, block_keys, block_values, allowed):
        run_top, run_total, summed = running
        scores = (
            jnp.einsum("qhgd,khd->hgqk", query_all, block_keys, preferred_element_type=jnp.float32)
            * score_scale
        )
        scores = jnp.where(allowed, scores, NEG)
        new_top = jnp.maximum(run_top, jnp.max(scores, axis=-1, keepdims=True))
        weights = jnp.where(allowed, jnp.exp(scores - new_top), 0.0).astype(jnp.bfloat16)
        shrink = jnp.exp(run_top - new_top)
        run_total = run_total * shrink + jnp.sum(
            weights.astype(jnp.float32), axis=-1, keepdims=True
        )
        summed = summed * shrink + jnp.einsum(
            "hgqk,khd->hgqd", weights, block_values, preferred_element_type=jnp.float32
        )
        return (new_top, run_total, summed)

    shard_rows = key_cache.shape[0]
    block_rows = shard_rows // 8
    key_blocks = key_cache.reshape(8, block_rows, KV_HEADS, HEAD_DIM)
    value_blocks = value_cache.reshape(8, block_rows, KV_HEADS, HEAD_DIM)
    first_block = pair_side * 8
    stride = 1
    needed = (cache_length + block_rows - 1) // block_rows
    live_blocks = jnp.clip((needed - first_block + stride - 1) // stride, 0, 8)

    def cache_step(block_index, running):
        block_keys = lax.dynamic_index_in_dim(key_blocks, block_index, 0, keepdims=False)
        block_values = lax.dynamic_index_in_dim(value_blocks, block_index, 0, keepdims=False)
        first_slot = (first_block + stride * block_index) * block_rows
        allowed = first_slot + jnp.arange(block_rows, dtype=jnp.int32) < cache_length
        allowed = jnp.broadcast_to(allowed[None, :], (tree_size, block_rows))
        return attend(running, block_keys, block_values, allowed)

    initial = (
        jnp.full((KV_HEADS, group_size, tree_size, 1), NEG, jnp.float32),
        jnp.zeros((KV_HEADS, group_size, tree_size, 1), jnp.float32),
        jnp.zeros((KV_HEADS, group_size, tree_size, HEAD_DIM), jnp.float32),
    )
    running = lax.fori_loop(0, live_blocks, cache_step, initial)
    running = attend(
        running, key_heads, new_values.reshape(half_rows, KV_HEADS, HEAD_DIM), own_cols
    )
    run_top, run_total, summed = running
    far_top, far_total, far_sum = (
        swapped(run_top[:, :, half_rows:].astype(jnp.bfloat16), "tp", 0).astype(jnp.float32),
        swapped(run_total[:, :, half_rows:].astype(jnp.bfloat16), "tp", 0).astype(jnp.float32),
        swapped(summed[:, :, half_rows:].astype(jnp.bfloat16), "tp", 0).astype(jnp.float32),
    )
    near_top = run_top[:, :, :half_rows]
    joint_top = jnp.maximum(near_top, far_top)
    near_scale = jnp.exp(near_top - joint_top)
    far_scale = jnp.exp(far_top - joint_top)
    denominator = run_total[:, :, :half_rows] * near_scale + far_total * far_scale
    merged = (summed[:, :, :half_rows] * near_scale + far_sum * far_scale) / denominator
    attended = jnp.transpose(merged, (2, 0, 1, 3)).reshape(half_rows, q_width).astype(jnp.bfloat16)
    leaf_pick = (node_ids == leaf_index).astype(jnp.float32)
    leaf_row = jnp.dot(leaf_pick, reached, precision=lax.Precision.HIGHEST)
    out_depths = (pair_side * half_rows + local_ids).astype(jnp.float32)
    chosen = leaf_row[None, :] * (node_depth[None, :] == out_depths[:, None]).astype(jnp.float32)
    chosen = jnp.dot(chosen, reorder.T, precision=lax.Precision.HIGHEST)
    fresh_all = jnp.concatenate([fresh_own, fresh_other], axis=0)
    accepted_kv = jnp.dot(
        chosen.astype(jnp.bfloat16), fresh_all, preferred_element_type=jnp.float32
    ).astype(jnp.bfloat16)
    levels = lax.axis_size("req") // SIDE
    places = SIDE * tp_count
    attn_slice = feature_slices(attended, 0)
    projected = jnp.dot(attn_slice, out_full, preferred_element_type=jnp.float32)
    projected = projected.astype(jnp.bfloat16).reshape(levels, places * half_rows, -1)
    projected = exchange(projected, "level", "lead", 1)
    projected = jnp.sum(projected.astype(jnp.float32), axis=0).astype(jnp.bfloat16)
    projected = exchange(projected.reshape(places, half_rows, -1), "place", "lead", 2)
    own_projected = jnp.transpose(
        projected.reshape(SIDE, tp_count, half_rows, -1), (2, 1, 0, 3)
    ).reshape(half_rows, -1)
    residual = (hidden_in.astype(jnp.float32) + own_projected.astype(jnp.float32)).astype(
        jnp.bfloat16
    )
    residual_wide = residual.astype(jnp.float32)
    mean_sq = jnp.mean(residual_wide * residual_wide, axis=-1, keepdims=True)
    normed = (residual_wide * lax.rsqrt(mean_sq + EPS) * post_gain.astype(jnp.float32)).astype(
        jnp.bfloat16
    )
    normed_slice = feature_slices(normed, 3)
    sums = jnp.dot(normed_slice, gate_up_full, preferred_element_type=jnp.float32)
    sums = sums.astype(jnp.bfloat16).reshape(levels, places * half_rows, -1)
    sums = jnp.sum(exchange(sums, "level", "lead", 4).astype(jnp.float32), axis=0)
    hidden_width = sums.shape[1] // 2
    hidden = (jax.nn.silu(sums[:, :hidden_width]) * sums[:, hidden_width:]).astype(jnp.bfloat16)
    hidden_all = exchange(hidden, "level", "copy", 5).reshape(-1, hidden_width)
    partial_out = jnp.dot(hidden_all, down_full, preferred_element_type=jnp.float32)
    partial_out = partial_out.astype(jnp.bfloat16).reshape(levels, places, half_rows, -1)
    paired_sum = exchange(partial_out, "place", "inner", 6).astype(jnp.float32)
    paired_sum = jnp.sum(paired_sum, axis=0).astype(jnp.bfloat16)
    mlp_own = exchange(paired_sum, "level", "lead", 7)
    mlp_own = jnp.transpose(mlp_own, (1, 0, 2)).reshape(half_rows, -1).astype(jnp.float32)
    layer_out = (residual_wide + mlp_own).astype(jnp.bfloat16)
    return (layer_out, accepted_kv)


def solution(mesh):
    in_specs = (
        P(("req", "tp"), None),
        P(("req", "tp"), None),
        P(("req", "tp"), None),
        P(("req", "tp"), None),
        P(("req", "tp"), None),
        P(("req", "tp"), None),
        P(),
        P(),
        P(),
        P(),
        P(),
        P(),
        P("req", "tp"),
        P("req", "tp"),
        P("req", "tp"),
        P("tp", "req"),
    )
    out_specs = (P(("req", "tp"), None), P(("req", "tp"), None))
    return jax.shard_map(
        per_device, mesh=mesh, in_specs=in_specs, out_specs=out_specs, check_vma=False
    )
```

```python
import functools

import jax
import jax.numpy as jnp
from jax import lax
from jax.experimental import pallas as pl
from jax.experimental.pallas import tpu as pltpu
from jax.sharding import PartitionSpec as P

HEADS = 32
KV_HEADS = 8
HEAD_DIM = 128


NEG = -1e30
EPS = 1e-06
ROPE_BASE = 1000000.0


def swapped(value, axis, bit):
    mask = 2**bit
    pairs = [(source, source ^ mask) for source in range(lax.axis_size(axis))]
    return lax.ppermute(value, axis, pairs)


def head_norm(values, gain_vec):
    mean_sq = jnp.mean(values * values, axis=-1, keepdims=True)
    return values * lax.rsqrt(mean_sq + EPS) * gain_vec.astype(jnp.float32)


def rotate(values, position):
    head_width = values.shape[-1]
    half_width = head_width // 2
    frequency = ROPE_BASE ** (-2.0 * jnp.arange(half_width, dtype=jnp.float32) / head_width)
    angles = position[:, None] * frequency[None, :]
    cosine = jnp.cos(angles)[:, None, :]
    sine_part = jnp.sin(angles)[:, None, :]
    front_half = values[..., :half_width]
    back_half = values[..., half_width:]
    return jnp.concatenate(
        [front_half * cosine - back_half * sine_part, back_half * cosine + front_half * sine_part],
        axis=-1,
    )


SIDE = 2
MESH = pl.DeviceIdType.MESH
ANY = pl.BlockSpec(memory_space=pl.ANY)


def meet(peers):
    barrier = pltpu.get_barrier_semaphore()
    for peer in peers:
        pl.semaphore_signal(barrier, inc=1, device_id=peer, device_id_type=MESH)
    pl.semaphore_wait(barrier, len(peers))


def remote(source, target, send_sem, recv_sem, peer):
    return pltpu.make_async_remote_copy(
        src_ref=source,
        dst_ref=target,
        send_sem=send_sem,
        recv_sem=recv_sem,
        device_id=peer,
        device_id_type=MESH,
    )


def exchange_kernel(along, mode, rows_ref, out_ref, send_sem, recv_sem, own_sem):
    tp_count = lax.axis_size("tp")
    req, tp = lax.axis_index("req"), lax.axis_index("tp")
    level, side = req // SIDE, req % SIDE
    if along == "level":
        count, mine = lax.axis_size("req") // SIDE, level
    else:
        count, mine = SIDE * tp_count, side * tp_count + tp

    def device(index):
        if along == "level":
            return {"req": index * SIDE + side, "tp": tp}
        return {"req": level * SIDE + index // tp_count, "tp": index % tp_count}

    def part(index):
        if mode == "copy":
            return rows_ref
        if mode == "inner":
            return rows_ref.at[:, index]
        return rows_ref.at[index]

    others = [(mine + step) % count for step in range(1, count)]
    meet([device(index) for index in others])
    copies = [
        remote(part(index), out_ref.at[mine], send_sem.at[at], recv_sem.at[at], device(index))
        for at, index in enumerate(others)
    ]
    for copy in copies:
        copy.start()
    own = pltpu.make_async_copy(part(mine), out_ref.at[mine], own_sem)
    own.start()
    for copy in copies:
        copy.wait()
    own.wait()


def exchange(rows, along, mode, collective_id):
    count = lax.axis_size("req") // SIDE if along == "level" else SIDE * lax.axis_size("tp")
    if mode == "copy":
        part_shape = rows.shape
    elif mode == "inner":
        part_shape = rows.shape[:1] + rows.shape[2:]
    else:
        part_shape = rows.shape[1:]
    return pl.pallas_call(
        functools.partial(exchange_kernel, along, mode),
        out_shape=jax.ShapeDtypeStruct((count, *part_shape), rows.dtype),
        in_specs=[ANY],
        out_specs=ANY,
        scratch_shapes=[
            pltpu.SemaphoreType.DMA((count - 1,)),
            pltpu.SemaphoreType.DMA((count - 1,)),
            pltpu.SemaphoreType.DMA,
        ],
        compiler_params=pltpu.CompilerParams(collective_id=collective_id, has_side_effects=True),
    )(rows)


def slices_kernel(
    rows_ref, out_ref, send_level, recv_level, send_far, recv_far, send_core, recv_core, own_sem
):
    tp_count = lax.axis_size("tp")
    levels = lax.axis_size("req") // SIDE
    req, tp = lax.axis_index("req"), lax.axis_index("tp")
    level, side = req // SIDE, req % SIDE
    place = side * tp_count + tp
    core, chip = tp % 2, place // 2
    chips = SIDE * tp_count // 2
    width = rows_ref.shape[1] // levels

    def columns(index):
        return rows_ref.at[:, pl.ds(pl.multiple_of(index * width, width), width)]

    def chip_place(index):
        return index * 2 + core

    def device(at):
        return {"req": level * SIDE + at // tp_count, "tp": at % tp_count}

    level_ids = [(level + step) % levels for step in range(1, levels)]
    level_devices = [{"req": index * SIDE + side, "tp": tp} for index in level_ids]
    far_devices = [device(chip_place((chip + step) % chips)) for step in range(1, chips)]
    core_device = device(chip * 2 + 1 - core)
    meet(level_devices + far_devices + [core_device])
    first = [
        remote(columns(index), out_ref.at[level, place], send_level.at[at], recv_level.at[at], peer)
        for at, (index, peer) in enumerate(zip(level_ids, level_devices))
    ]
    for copy in first:
        copy.start()
    own = pltpu.make_async_copy(columns(level), out_ref.at[level, place], own_sem)
    own.start()
    far, near = [], []
    for step in range(levels):
        source_level = (level - step + levels) % levels
        target = out_ref.at[source_level, place]
        if step > 0:
            first[step - 1].wait_recv()
        source = columns(level) if step == 0 else target
        for peer in far_devices:
            at = len(far)
            copy = remote(source, target, send_far.at[at], recv_far.at[at], peer)
            copy.start()
            far.append(copy)
        at = len(near)
        copy = remote(source, target, send_core.at[at], recv_core.at[at], core_device)
        copy.start()
        near.append(copy)
    for step in range(levels):
        source_level = (level - step + levels) % levels
        for hop in range(1, chips):
            far[step * (chips - 1) + hop - 1].wait_recv()
            landed = out_ref.at[source_level, chip_place((chip - hop + chips) % chips)]
            at = len(near)
            copy = remote(landed, landed, send_core.at[at], recv_core.at[at], core_device)
            copy.start()
            near.append(copy)
    own.wait()
    for copy in near:
        copy.wait()
    for copy in first + far:
        copy.wait_send()


def feature_slices(rows, collective_id):
    levels = lax.axis_size("req") // SIDE
    places = SIDE * lax.axis_size("tp")
    width = rows.shape[1] // levels
    chips = places // 2
    gathered = pl.pallas_call(
        slices_kernel,
        out_shape=jax.ShapeDtypeStruct((levels, places, rows.shape[0], width), rows.dtype),
        in_specs=[ANY],
        out_specs=ANY,
        scratch_shapes=[
            pltpu.SemaphoreType.DMA((levels - 1,)),
            pltpu.SemaphoreType.DMA((levels - 1,)),
            pltpu.SemaphoreType.DMA((levels * (chips - 1),)),
            pltpu.SemaphoreType.DMA((levels * (chips - 1),)),
            pltpu.SemaphoreType.DMA((levels * chips,)),
            pltpu.SemaphoreType.DMA((levels * chips,)),
            pltpu.SemaphoreType.DMA,
        ],
        compiler_params=pltpu.CompilerParams(collective_id=collective_id, has_side_effects=True),
    )(rows)
    return gathered.reshape(-1, width)


def paired_halves(shard, axis):
    side = lax.axis_index("req") % SIDE
    half = shard.shape[axis] // 2
    kept = lax.dynamic_slice_in_dim(shard, side * half, half, axis)
    sent = lax.dynamic_slice_in_dim(shard, (1 - side) * half, half, axis)
    return kept, sent


def joined(kept, received, axis):
    side = lax.axis_index("req") % SIDE
    low = jnp.where(side == 0, kept, received)
    high = jnp.where(side == 0, received, kept)
    return jnp.concatenate([low, high], axis=axis)


def attention_kernel(
    limit_ref, query_ref, key_ref, value_ref, fresh_key_ref, fresh_value_ref, allowed_ref,
    top_ref, total_ref, sum_ref,
):
    group_size = query_ref.shape[1] // HEAD_DIM
    query = jnp.concatenate(
        [query_ref[:, at * HEAD_DIM : (at + 1) * HEAD_DIM] for at in range(group_size)], axis=0
    )
    score_scale = HEAD_DIM ** (-0.5)
    limit = limit_ref[0]
    chunk = key_ref.shape[0] // 4

    def score(keys):
        return (
            lax.dot_general(
                query, keys, (((1,), (1,)), ((), ())), preferred_element_type=jnp.float32
            )
            * score_scale
        )

    def weigh(scores, top, allowed):
        weights = jnp.where(allowed, jnp.exp(scores - top), 0.0).astype(jnp.bfloat16)
        return weights, jnp.sum(weights.astype(jnp.float32), axis=-1, keepdims=True)

    allowed = jnp.concatenate([allowed_ref[...]] * group_size, axis=0) > 0.5
    scores = jnp.where(allowed, score(fresh_key_ref[...]), NEG)
    top = jnp.max(scores, axis=-1, keepdims=True)
    weights, total = weigh(scores, top, allowed)
    summed = jnp.dot(weights, fresh_value_ref[...], preferred_element_type=jnp.float32)

    def step(index, running):
        top, total, summed = running
        start = pl.multiple_of(index * chunk, chunk)
        keys = key_ref[pl.ds(start, chunk), :]
        values = value_ref[pl.ds(start, chunk), :]
        allowed = lax.broadcasted_iota(jnp.int32, (query.shape[0], chunk), 1) + start < limit
        scores = jnp.where(allowed, score(keys), NEG)
        new_top = jnp.maximum(top, jnp.max(scores, axis=-1, keepdims=True))
        weights, chunk_total = weigh(scores, new_top, allowed)
        shrink = jnp.exp(top - new_top)
        summed = summed * shrink + jnp.dot(weights, values, preferred_element_type=jnp.float32)
        return new_top, total * shrink + chunk_total, summed

    live = jnp.clip((limit + chunk - 1) // chunk, 0, 4)
    top, total, summed = lax.fori_loop(0, live, step, (top, total, summed))
    top_ref[0] = top
    total_ref[0] = total
    sum_ref[0] = summed


def attend(limit, query, keys, values, fresh_keys, fresh_values, allowed):
    rows, fresh_rows, cached_rows = query.shape[0], fresh_keys.shape[0], keys.shape[0]
    group_size = HEADS // KV_HEADS
    group_rows = rows * group_size

    def columns(block_rows, width):
        return pl.BlockSpec((block_rows, width), lambda head, limit_ref: (0, head))

    def lead(width):
        return pl.BlockSpec((1, group_rows, width), lambda head, limit_ref: (head, 0, 0))

    results = pl.pallas_call(
        attention_kernel,
        out_shape=[
            jax.ShapeDtypeStruct((KV_HEADS, group_rows, width), jnp.float32)
            for width in (1, 1, HEAD_DIM)
        ],
        grid_spec=pltpu.PrefetchScalarGridSpec(
            num_scalar_prefetch=1,
            grid=(KV_HEADS,),
            in_specs=[
                columns(rows, group_size * HEAD_DIM),
                columns(cached_rows, HEAD_DIM),
                columns(cached_rows, HEAD_DIM),
                columns(fresh_rows, HEAD_DIM),
                columns(fresh_rows, HEAD_DIM),
                pl.BlockSpec((rows, fresh_rows), lambda head, limit_ref: (0, 0)),
            ],
            out_specs=[lead(1), lead(1), lead(HEAD_DIM)],
        ),
        compiler_params=pltpu.CompilerParams(vmem_limit_bytes=32 * 2**20),
        cost_estimate=pl.CostEstimate(
            flops=4 * group_rows * cached_rows * KV_HEADS * HEAD_DIM,
            bytes_accessed=4 * cached_rows * KV_HEADS * HEAD_DIM,
            transcendentals=group_rows * cached_rows * KV_HEADS,
        ),
    )(limit, query, keys, values, fresh_keys, fresh_values, allowed)
    return [
        result.reshape(KV_HEADS, group_size, rows, result.shape[2]) for result in results
    ]


def ancestors(parent_row):
    node_count = parent_row.shape[0]
    node_ids = jnp.arange(node_count, dtype=jnp.int32)
    identity_mat = (node_ids[:, None] == node_ids[None, :]).astype(jnp.float32)
    parent_mat = (parent_row[:, None] == node_ids[None, :]).astype(jnp.float32) * (
        1.0 - identity_mat
    )
    reached = jnp.minimum(identity_mat + parent_mat, 1.0)
    for sweep in range(node_count.bit_length()):
        reached = jnp.minimum(jnp.dot(reached, reached, precision=lax.Precision.HIGHEST), 1.0)
    return reached


def per_device(
    hidden_in,
    queries,
    new_keys,
    new_values,
    key_cache,
    value_cache,
    cache_lengths,
    parent_ids,
    accepted_leaf,
    query_gain,
    key_gain,
    post_gain,
    out_weight,
    gate_weight,
    up_weight,
    down_weight,
):
    half_rows = queries.shape[0]
    out_kept, out_sent = paired_halves(out_weight, 1)
    out_received = swapped(out_sent, "req", 0)
    gate_kept, gate_sent = paired_halves(gate_weight, 1)
    up_kept, up_sent = paired_halves(up_weight, 1)
    gate_up_received = swapped(jnp.concatenate([gate_sent, up_sent], axis=1), "req", 0)
    gate_up_kept = jnp.concatenate([gate_kept, up_kept], axis=1)
    down_kept, down_sent = paired_halves(down_weight, 0)
    down_received = swapped(down_sent, "req", 0)
    out_full = joined(out_kept, out_received, 0)
    gate_up_full = joined(gate_up_kept, gate_up_received, 0)
    down_full = joined(down_kept, down_received, 1)
    tree_size = 2 * half_rows
    kv_width = new_keys.shape[1]
    q_width = queries.shape[1]
    tp_count = lax.axis_size("tp")
    device = lax.axis_index(("req", "tp"))
    request = device // 2
    pair_side = lax.axis_index("tp") % 2
    cache_length = lax.dynamic_index_in_dim(cache_lengths, request, 0, keepdims=False)
    parent_row = lax.dynamic_index_in_dim(parent_ids, request, 0, keepdims=False)
    leaf_index = lax.dynamic_index_in_dim(accepted_leaf, request, 0, keepdims=False)
    reached = ancestors(parent_row)
    node_depth = jnp.sum(reached, axis=1) - 1.0
    node_ids = jnp.arange(tree_size, dtype=jnp.int32)
    local_ids = jnp.arange(half_rows, dtype=jnp.int32)
    node_order = jnp.concatenate(
        [pair_side * half_rows + local_ids, (1 - pair_side) * half_rows + local_ids]
    )
    reorder = (node_order[:, None] == node_ids[None, :]).astype(jnp.float32)
    reached_rows = jnp.dot(reorder, reached, precision=lax.Precision.HIGHEST)
    own_cols = jnp.dot(reached_rows, reorder[:half_rows].T, precision=lax.Precision.HIGHEST) > 0.5
    own_depth = jnp.dot(reorder[:half_rows], node_depth, precision=lax.Precision.HIGHEST)
    position = cache_length.astype(jnp.float32) + own_depth
    query_heads = rotate(
        head_norm(queries.astype(jnp.float32).reshape(half_rows, HEADS, HEAD_DIM), query_gain),
        position,
    ).astype(jnp.bfloat16)
    key_heads = rotate(
        head_norm(new_keys.astype(jnp.float32).reshape(half_rows, KV_HEADS, HEAD_DIM), key_gain),
        position,
    ).astype(jnp.bfloat16)
    query_own = query_heads.reshape(half_rows, q_width)
    fresh_own = jnp.concatenate([key_heads.reshape(half_rows, kv_width), new_values], axis=1)
    query_other, fresh_other = swapped((query_own, fresh_own), "tp", 0)
    query_all = jnp.concatenate([query_own, query_other], axis=0)
    limit = (cache_length - pair_side * key_cache.shape[0]).reshape(1)
    run_top, run_total, summed = attend(
        limit,
        query_all,
        key_cache,
        value_cache,
        key_heads.reshape(half_rows, kv_width),
        new_values,
        own_cols.astype(jnp.float32),
    )
    far_top, far_total, far_sum = (
        swapped(run_top[:, :, half_rows:].astype(jnp.bfloat16), "tp", 0).astype(jnp.float32),
        swapped(run_total[:, :, half_rows:].astype(jnp.bfloat16), "tp", 0).astype(jnp.float32),
        swapped(summed[:, :, half_rows:].astype(jnp.bfloat16), "tp", 0).astype(jnp.float32),
    )
    near_top = run_top[:, :, :half_rows]
    joint_top = jnp.maximum(near_top, far_top)
    near_scale = jnp.exp(near_top - joint_top)
    far_scale = jnp.exp(far_top - joint_top)
    denominator = run_total[:, :, :half_rows] * near_scale + far_total * far_scale
    merged = (summed[:, :, :half_rows] * near_scale + far_sum * far_scale) / denominator
    attended = jnp.transpose(merged, (2, 0, 1, 3)).reshape(half_rows, q_width).astype(jnp.bfloat16)
    leaf_pick = (node_ids == leaf_index).astype(jnp.float32)
    leaf_row = jnp.dot(leaf_pick, reached, precision=lax.Precision.HIGHEST)
    out_depths = (pair_side * half_rows + local_ids).astype(jnp.float32)
    chosen = leaf_row[None, :] * (node_depth[None, :] == out_depths[:, None]).astype(jnp.float32)
    chosen = jnp.dot(chosen, reorder.T, precision=lax.Precision.HIGHEST)
    fresh_all = jnp.concatenate([fresh_own, fresh_other], axis=0)
    accepted_kv = jnp.dot(
        chosen.astype(jnp.bfloat16), fresh_all, preferred_element_type=jnp.float32
    ).astype(jnp.bfloat16)
    levels = lax.axis_size("req") // SIDE
    places = SIDE * tp_count
    attn_slice = feature_slices(attended, 0)
    projected = jnp.dot(attn_slice, out_full, preferred_element_type=jnp.float32)
    projected = projected.astype(jnp.bfloat16).reshape(levels, places * half_rows, -1)
    projected = exchange(projected, "level", "lead", 1)
    projected = jnp.sum(projected.astype(jnp.float32), axis=0).astype(jnp.bfloat16)
    projected = exchange(projected.reshape(places, half_rows, -1), "place", "lead", 2)
    own_projected = jnp.transpose(
        projected.reshape(SIDE, tp_count, half_rows, -1), (2, 1, 0, 3)
    ).reshape(half_rows, -1)
    residual = (hidden_in.astype(jnp.float32) + own_projected.astype(jnp.float32)).astype(
        jnp.bfloat16
    )
    residual_wide = residual.astype(jnp.float32)
    mean_sq = jnp.mean(residual_wide * residual_wide, axis=-1, keepdims=True)
    normed = (residual_wide * lax.rsqrt(mean_sq + EPS) * post_gain.astype(jnp.float32)).astype(
        jnp.bfloat16
    )
    normed_slice = feature_slices(normed, 3)
    sums = jnp.dot(normed_slice, gate_up_full, preferred_element_type=jnp.float32)
    sums = sums.astype(jnp.bfloat16).reshape(levels, places * half_rows, -1)
    sums = jnp.sum(exchange(sums, "level", "lead", 4).astype(jnp.float32), axis=0)
    hidden_width = sums.shape[1] // 2
    hidden = (jax.nn.silu(sums[:, :hidden_width]) * sums[:, hidden_width:]).astype(jnp.bfloat16)
    hidden_all = exchange(hidden, "level", "copy", 5).reshape(-1, hidden_width)
    partial_out = jnp.dot(hidden_all, down_full, preferred_element_type=jnp.float32)
    partial_out = partial_out.astype(jnp.bfloat16).reshape(levels, places, half_rows, -1)
    paired_sum = exchange(partial_out, "place", "inner", 6).astype(jnp.float32)
    paired_sum = jnp.sum(paired_sum, axis=0).astype(jnp.bfloat16)
    mlp_own = exchange(paired_sum, "level", "lead", 7)
    mlp_own = jnp.transpose(mlp_own, (1, 0, 2)).reshape(half_rows, -1).astype(jnp.float32)
    layer_out = (residual_wide + mlp_own).astype(jnp.bfloat16)
    return (layer_out, accepted_kv)


def solution(mesh):
    in_specs = (
        P(("req", "tp"), None),
        P(("req", "tp"), None),
        P(("req", "tp"), None),
        P(("req", "tp"), None),
        P(("req", "tp"), None),
        P(("req", "tp"), None),
        P(),
        P(),
        P(),
        P(),
        P(),
        P(),
        P("req", "tp"),
        P("req", "tp"),
        P("req", "tp"),
        P("tp", "req"),
    )
    out_specs = (P(("req", "tp"), None), P(("req", "tp"), None))
    return jax.shard_map(
        per_device, mesh=mesh, in_specs=in_specs, out_specs=out_specs, check_vma=False
    )
```

```python
import functools

import jax
import jax.numpy as jnp
from jax import lax
from jax.experimental import pallas as pl
from jax.experimental.pallas import tpu as pltpu
from jax.sharding import PartitionSpec as P

HEADS = 32
KV_HEADS = 8
HEAD_DIM = 128


NEG = -1e30
EPS = 1e-06
ROPE_BASE = 1000000.0


def swapped(value, axis, bit):
    mask = 2**bit
    pairs = [(source, source ^ mask) for source in range(lax.axis_size(axis))]
    return lax.ppermute(value, axis, pairs)


def head_norm(values, gain_vec):
    mean_sq = jnp.mean(values * values, axis=-1, keepdims=True)
    return values * lax.rsqrt(mean_sq + EPS) * gain_vec.astype(jnp.float32)


def rotate(values, position):
    head_width = values.shape[-1]
    half_width = head_width // 2
    frequency = ROPE_BASE ** (-2.0 * jnp.arange(half_width, dtype=jnp.float32) / head_width)
    angles = position[:, None] * frequency[None, :]
    cosine = jnp.cos(angles)[:, None, :]
    sine_part = jnp.sin(angles)[:, None, :]
    front_half = values[..., :half_width]
    back_half = values[..., half_width:]
    return jnp.concatenate(
        [front_half * cosine - back_half * sine_part, back_half * cosine + front_half * sine_part],
        axis=-1,
    )


SIDE = 2
MESH = pl.DeviceIdType.MESH
ANY = pl.BlockSpec(memory_space=pl.ANY)


def meet(peers):
    barrier = pltpu.get_barrier_semaphore()
    for peer in peers:
        pl.semaphore_signal(barrier, inc=1, device_id=peer, device_id_type=MESH)
    pl.semaphore_wait(barrier, len(peers))


def remote(source, target, send_sem, recv_sem, peer):
    return pltpu.make_async_remote_copy(
        src_ref=source,
        dst_ref=target,
        send_sem=send_sem,
        recv_sem=recv_sem,
        device_id=peer,
        device_id_type=MESH,
    )


def line_of(along):
    tp_count = lax.axis_size("tp")
    req, tp = lax.axis_index("req"), lax.axis_index("tp")
    level, side = req // SIDE, req % SIDE
    if along == "level":
        return (
            lax.axis_size("req") // SIDE,
            level,
            lambda index: {"req": index * SIDE + side, "tp": tp},
        )
    return (
        SIDE * tp_count,
        side * tp_count + tp,
        lambda index: {"req": level * SIDE + index // tp_count, "tp": index % tp_count},
    )


def exchange_kernel(along, rows_ref, out_ref, send_sem, recv_sem, own_sem):
    count, mine, device = line_of(along)

    def part(index):
        return rows_ref.at[index]

    others = [(mine + step) % count for step in range(1, count)]
    meet([device(index) for index in others])
    copies = [
        remote(part(index), out_ref.at[mine], send_sem.at[at], recv_sem.at[at], device(index))
        for at, index in enumerate(others)
    ]
    for copy in copies:
        copy.start()
    own = pltpu.make_async_copy(part(mine), out_ref.at[mine], own_sem)
    own.start()
    for copy in copies:
        copy.wait()
    own.wait()


def exchange(rows, along, collective_id):
    count = lax.axis_size("req") // SIDE if along == "level" else SIDE * lax.axis_size("tp")
    part_shape = rows.shape[1:]
    return pl.pallas_call(
        functools.partial(exchange_kernel, along),
        out_shape=jax.ShapeDtypeStruct((count, *part_shape), rows.dtype),
        in_specs=[ANY],
        out_specs=ANY,
        scratch_shapes=[
            pltpu.SemaphoreType.DMA((count - 1,)),
            pltpu.SemaphoreType.DMA((count - 1,)),
            pltpu.SemaphoreType.DMA,
        ],
        compiler_params=pltpu.CompilerParams(collective_id=collective_id, has_side_effects=True),
    )(rows)


def reduce_kernel(
    along, mode, rows_ref, out_ref, landed, held,
    pair_send, pair_recv, far_send, far_recv, last_send, last_recv, own_sems,
):
    count, mine, device = line_of(along)
    half, place, parity = count // 2, mine // 2, mine % 2
    depth = landed.shape[1]
    piece = depth // 2

    def part(index, start, size):
        if mode == "inner":
            return rows_ref.at[pl.ds(start, size), index]
        return rows_ref.at[index, pl.ds(start, size)]

    order = [(place + step) % half for step in range(1, half)]
    pair = device(place * 2 + 1 - parity)
    far_devices = [device(index * 2 + parity) for index in order]
    meet(far_devices + [pair])
    inward, kept, outward = [], [], []
    for at, index in enumerate(order):
        for cut in range(2):
            copy = remote(
                part(index * 2 + 1 - parity, cut * piece, piece),
                landed.at[at, pl.ds(cut * piece, piece)],
                pair_send.at[at * 2 + cut],
                pair_recv.at[at * 2 + cut],
                pair,
            )
            copy.start()
            inward.append(copy)
        copy = pltpu.make_async_copy(
            part(index * 2 + parity, 0, depth), held.at[at], own_sems.at[at + 1]
        )
        copy.start()
        kept.append(copy)
    last = remote(
        part(place * 2 + 1 - parity, 0, depth), out_ref.at[1], last_send, last_recv, pair
    )
    last.start()
    own = pltpu.make_async_copy(part(mine, 0, depth), out_ref.at[0], own_sems.at[0])
    own.start()
    for at, peer in enumerate(far_devices):
        kept[at].wait()
        for cut in range(2):
            inward[at * 2 + cut].wait_recv()

            @pl.loop(cut * piece, (cut + 1) * piece)
            def _(row):
                total = held[at, row].astype(jnp.float32) + landed[at, row].astype(jnp.float32)
                held[at, row] = total.astype(held.dtype)

            copy = remote(
                held.at[at, pl.ds(cut * piece, piece)],
                out_ref.at[at + 2, pl.ds(cut * piece, piece)],
                far_send.at[at * 2 + cut],
                far_recv.at[at * 2 + cut],
                peer,
            )
            copy.start()
            outward.append(copy)
    own.wait()
    last.wait()
    for copy in inward:
        copy.wait_send()
    for copy in outward:
        copy.wait()


def reduced(rows, along, mode, collective_id):
    count = lax.axis_size("req") // SIDE if along == "level" else SIDE * lax.axis_size("tp")
    half = count // 2
    if mode == "inner":
        part_shape = rows.shape[:1] + rows.shape[2:]
    else:
        part_shape = rows.shape[1:]
    parts = pl.pallas_call(
        functools.partial(reduce_kernel, along, mode),
        out_shape=jax.ShapeDtypeStruct((half + 1, *part_shape), rows.dtype),
        in_specs=[ANY],
        out_specs=ANY,
        scratch_shapes=[
            pltpu.VMEM((half - 1, *part_shape), rows.dtype),
            pltpu.VMEM((half - 1, *part_shape), rows.dtype),
            pltpu.SemaphoreType.DMA((2 * (half - 1),)),
            pltpu.SemaphoreType.DMA((2 * (half - 1),)),
            pltpu.SemaphoreType.DMA((2 * (half - 1),)),
            pltpu.SemaphoreType.DMA((2 * (half - 1),)),
            pltpu.SemaphoreType.DMA,
            pltpu.SemaphoreType.DMA,
            pltpu.SemaphoreType.DMA((half,)),
        ],
        compiler_params=pltpu.CompilerParams(
            collective_id=collective_id, has_side_effects=True, vmem_limit_bytes=40 * 2**20
        ),
    )(rows)
    return jnp.sum(parts.astype(jnp.float32), axis=0)


def gather_kernel(rows_ref, out_ref, far_send, far_recv, near_send, near_recv, own_sem):
    count, mine, device = line_of("level")
    half, place, parity = count // 2, mine // 2, mine % 2
    pair = device(place * 2 + 1 - parity)
    order = [(place + step) % half for step in range(1, half)]
    far_devices = [device(index * 2 + parity) for index in order]
    meet(far_devices + [pair])
    far, near = [], []
    for cut in range(2):
        for peer in far_devices:
            at = len(far)
            copy = remote(
                rows_ref.at[cut], out_ref.at[mine, cut], far_send.at[at], far_recv.at[at], peer
            )
            copy.start()
            far.append(copy)
    own = pltpu.make_async_copy(rows_ref, out_ref.at[mine], own_sem)
    own.start()
    for cut in range(2):
        at = len(near)
        copy = remote(
            rows_ref.at[cut], out_ref.at[mine, cut], near_send.at[at], near_recv.at[at], pair
        )
        copy.start()
        near.append(copy)
    for cut in range(2):
        for step in range(1, half):
            far[cut * (half - 1) + step - 1].wait_recv()
            landed = out_ref.at[((place - step + half) % half) * 2 + parity, cut]
            at = len(near)
            copy = remote(landed, landed, near_send.at[at], near_recv.at[at], pair)
            copy.start()
            near.append(copy)
    own.wait()
    for copy in near:
        copy.wait()
    for copy in far:
        copy.wait_send()


def gathered_levels(rows, collective_id):
    count = lax.axis_size("req") // SIDE
    half = count // 2
    rows = rows.reshape(2, rows.shape[0] // 2, rows.shape[1])
    return pl.pallas_call(
        gather_kernel,
        out_shape=jax.ShapeDtypeStruct((count, *rows.shape), rows.dtype),
        in_specs=[ANY],
        out_specs=ANY,
        scratch_shapes=[
            pltpu.SemaphoreType.DMA((2 * (half - 1),)),
            pltpu.SemaphoreType.DMA((2 * (half - 1),)),
            pltpu.SemaphoreType.DMA((2 * half,)),
            pltpu.SemaphoreType.DMA((2 * half,)),
            pltpu.SemaphoreType.DMA,
        ],
        compiler_params=pltpu.CompilerParams(collective_id=collective_id, has_side_effects=True),
    )(rows)


def slices_kernel(
    rows_ref, out_ref, send_level, recv_level, send_far, recv_far, send_core, recv_core, own_sem
):
    tp_count = lax.axis_size("tp")
    levels = lax.axis_size("req") // SIDE
    req, tp = lax.axis_index("req"), lax.axis_index("tp")
    level, side = req // SIDE, req % SIDE
    place = side * tp_count + tp
    core, chip = tp % 2, place // 2
    chips = SIDE * tp_count // 2
    width = rows_ref.shape[1] // levels

    def columns(index):
        return rows_ref.at[:, pl.ds(pl.multiple_of(index * width, width), width)]

    def chip_place(index):
        return index * 2 + core

    def device(at):
        return {"req": level * SIDE + at // tp_count, "tp": at % tp_count}

    level_ids = [(level + step) % levels for step in range(1, levels)]
    level_devices = [{"req": index * SIDE + side, "tp": tp} for index in level_ids]
    far_devices = [device(chip_place((chip + step) % chips)) for step in range(1, chips)]
    core_device = device(chip * 2 + 1 - core)
    meet(level_devices + far_devices + [core_device])
    first = [
        remote(columns(index), out_ref.at[level, place], send_level.at[at], recv_level.at[at], peer)
        for at, (index, peer) in enumerate(zip(level_ids, level_devices))
    ]
    for copy in first:
        copy.start()
    own = pltpu.make_async_copy(columns(level), out_ref.at[level, place], own_sem)
    own.start()
    far, near = [], []
    for step in range(levels):
        source_level = (level - step + levels) % levels
        target = out_ref.at[source_level, place]
        if step > 0:
            first[step - 1].wait_recv()
        source = columns(level) if step == 0 else target
        for peer in far_devices:
            at = len(far)
            copy = remote(source, target, send_far.at[at], recv_far.at[at], peer)
            copy.start()
            far.append(copy)
        at = len(near)
        copy = remote(source, target, send_core.at[at], recv_core.at[at], core_device)
        copy.start()
        near.append(copy)
    for step in range(levels):
        source_level = (level - step + levels) % levels
        for hop in range(1, chips):
            far[step * (chips - 1) + hop - 1].wait_recv()
            landed = out_ref.at[source_level, chip_place((chip - hop + chips) % chips)]
            at = len(near)
            copy = remote(landed, landed, send_core.at[at], recv_core.at[at], core_device)
            copy.start()
            near.append(copy)
    own.wait()
    for copy in near:
        copy.wait()
    for copy in first + far:
        copy.wait_send()


def feature_slices(rows, collective_id):
    levels = lax.axis_size("req") // SIDE
    places = SIDE * lax.axis_size("tp")
    width = rows.shape[1] // levels
    chips = places // 2
    gathered = pl.pallas_call(
        slices_kernel,
        out_shape=jax.ShapeDtypeStruct((levels, places, rows.shape[0], width), rows.dtype),
        in_specs=[ANY],
        out_specs=ANY,
        scratch_shapes=[
            pltpu.SemaphoreType.DMA((levels - 1,)),
            pltpu.SemaphoreType.DMA((levels - 1,)),
            pltpu.SemaphoreType.DMA((levels * (chips - 1),)),
            pltpu.SemaphoreType.DMA((levels * (chips - 1),)),
            pltpu.SemaphoreType.DMA((levels * chips,)),
            pltpu.SemaphoreType.DMA((levels * chips,)),
            pltpu.SemaphoreType.DMA,
        ],
        compiler_params=pltpu.CompilerParams(collective_id=collective_id, has_side_effects=True),
    )(rows)
    return gathered.reshape(-1, width)


def paired_halves(shard, axis):
    side = lax.axis_index("req") % SIDE
    half = shard.shape[axis] // 2
    kept = lax.dynamic_slice_in_dim(shard, side * half, half, axis)
    sent = lax.dynamic_slice_in_dim(shard, (1 - side) * half, half, axis)
    return kept, sent


def joined(kept, received, axis):
    side = lax.axis_index("req") % SIDE
    low = jnp.where(side == 0, kept, received)
    high = jnp.where(side == 0, received, kept)
    return jnp.concatenate([low, high], axis=axis)


def attention_kernel(
    limit_ref, query_ref, key_ref, value_ref, fresh_key_ref, fresh_value_ref, allowed_ref,
    top_ref, total_ref, sum_ref,
):
    group_size = query_ref.shape[1] // HEAD_DIM
    query = jnp.concatenate(
        [query_ref[:, at * HEAD_DIM : (at + 1) * HEAD_DIM] for at in range(group_size)], axis=0
    )
    score_scale = HEAD_DIM ** (-0.5)
    limit = limit_ref[0]
    chunk = key_ref.shape[0] // 4

    def score(keys):
        return (
            lax.dot_general(
                query, keys, (((1,), (1,)), ((), ())), preferred_element_type=jnp.float32
            )
            * score_scale
        )

    def weigh(scores, top, allowed):
        weights = jnp.where(allowed, jnp.exp(scores - top), 0.0).astype(jnp.bfloat16)
        return weights, jnp.sum(weights.astype(jnp.float32), axis=-1, keepdims=True)

    allowed = jnp.concatenate([allowed_ref[...]] * group_size, axis=0) > 0.5
    scores = jnp.where(allowed, score(fresh_key_ref[...]), NEG)
    top = jnp.max(scores, axis=-1, keepdims=True)
    weights, total = weigh(scores, top, allowed)
    summed = jnp.dot(weights, fresh_value_ref[...], preferred_element_type=jnp.float32)

    def step(index, running):
        top, total, summed = running
        start = pl.multiple_of(index * chunk, chunk)
        keys = key_ref[pl.ds(start, chunk), :]
        values = value_ref[pl.ds(start, chunk), :]
        allowed = lax.broadcasted_iota(jnp.int32, (query.shape[0], chunk), 1) + start < limit
        scores = jnp.where(allowed, score(keys), NEG)
        new_top = jnp.maximum(top, jnp.max(scores, axis=-1, keepdims=True))
        weights, chunk_total = weigh(scores, new_top, allowed)
        shrink = jnp.exp(top - new_top)
        summed = summed * shrink + jnp.dot(weights, values, preferred_element_type=jnp.float32)
        return new_top, total * shrink + chunk_total, summed

    live = jnp.clip((limit + chunk - 1) // chunk, 0, 4)
    top, total, summed = lax.fori_loop(0, live, step, (top, total, summed))
    top_ref[0] = top
    total_ref[0] = total
    sum_ref[0] = summed


def attend(limit, query, keys, values, fresh_keys, fresh_values, allowed):
    rows, fresh_rows, cached_rows = query.shape[0], fresh_keys.shape[0], keys.shape[0]
    group_size = HEADS // KV_HEADS
    group_rows = rows * group_size

    def columns(block_rows, width):
        return pl.BlockSpec((block_rows, width), lambda head, limit_ref: (0, head))

    def lead(width):
        return pl.BlockSpec((1, group_rows, width), lambda head, limit_ref: (head, 0, 0))

    results = pl.pallas_call(
        attention_kernel,
        out_shape=[
            jax.ShapeDtypeStruct((KV_HEADS, group_rows, width), jnp.float32)
            for width in (1, 1, HEAD_DIM)
        ],
        grid_spec=pltpu.PrefetchScalarGridSpec(
            num_scalar_prefetch=1,
            grid=(KV_HEADS,),
            in_specs=[
                columns(rows, group_size * HEAD_DIM),
                columns(cached_rows, HEAD_DIM),
                columns(cached_rows, HEAD_DIM),
                columns(fresh_rows, HEAD_DIM),
                columns(fresh_rows, HEAD_DIM),
                pl.BlockSpec((rows, fresh_rows), lambda head, limit_ref: (0, 0)),
            ],
            out_specs=[lead(1), lead(1), lead(HEAD_DIM)],
        ),
        compiler_params=pltpu.CompilerParams(vmem_limit_bytes=32 * 2**20),
        cost_estimate=pl.CostEstimate(
            flops=4 * group_rows * cached_rows * KV_HEADS * HEAD_DIM,
            bytes_accessed=4 * cached_rows * KV_HEADS * HEAD_DIM,
            transcendentals=group_rows * cached_rows * KV_HEADS,
        ),
    )(limit, query, keys, values, fresh_keys, fresh_values, allowed)
    return [
        result.reshape(KV_HEADS, group_size, rows, result.shape[2]) for result in results
    ]


def ancestors(parent_row):
    node_count = parent_row.shape[0]
    node_ids = jnp.arange(node_count, dtype=jnp.int32)
    identity_mat = (node_ids[:, None] == node_ids[None, :]).astype(jnp.float32)
    parent_mat = (parent_row[:, None] == node_ids[None, :]).astype(jnp.float32) * (
        1.0 - identity_mat
    )
    reached = jnp.minimum(identity_mat + parent_mat, 1.0)
    for sweep in range(node_count.bit_length()):
        reached = jnp.minimum(jnp.dot(reached, reached, precision=lax.Precision.HIGHEST), 1.0)
    return reached


def per_device(
    hidden_in,
    queries,
    new_keys,
    new_values,
    key_cache,
    value_cache,
    cache_lengths,
    parent_ids,
    accepted_leaf,
    query_gain,
    key_gain,
    post_gain,
    out_weight,
    gate_weight,
    up_weight,
    down_weight,
):
    half_rows = queries.shape[0]
    out_kept, out_sent = paired_halves(out_weight, 1)
    out_received = swapped(out_sent, "req", 0)
    gate_kept, gate_sent = paired_halves(gate_weight, 1)
    up_kept, up_sent = paired_halves(up_weight, 1)
    gate_up_received = swapped(jnp.concatenate([gate_sent, up_sent], axis=1), "req", 0)
    gate_up_kept = jnp.concatenate([gate_kept, up_kept], axis=1)
    down_kept, down_sent = paired_halves(down_weight, 0)
    out_full = joined(out_kept, out_received, 0)
    gate_up_full = joined(gate_up_kept, gate_up_received, 0)
    tree_size = 2 * half_rows
    kv_width = new_keys.shape[1]
    q_width = queries.shape[1]
    tp_count = lax.axis_size("tp")
    device = lax.axis_index(("req", "tp"))
    request = device // 2
    pair_side = lax.axis_index("tp") % 2
    cache_length = lax.dynamic_index_in_dim(cache_lengths, request, 0, keepdims=False)
    parent_row = lax.dynamic_index_in_dim(parent_ids, request, 0, keepdims=False)
    leaf_index = lax.dynamic_index_in_dim(accepted_leaf, request, 0, keepdims=False)
    reached = ancestors(parent_row)
    node_depth = jnp.sum(reached, axis=1) - 1.0
    node_ids = jnp.arange(tree_size, dtype=jnp.int32)
    local_ids = jnp.arange(half_rows, dtype=jnp.int32)
    node_order = jnp.concatenate(
        [pair_side * half_rows + local_ids, (1 - pair_side) * half_rows + local_ids]
    )
    reorder = (node_order[:, None] == node_ids[None, :]).astype(jnp.float32)
    reached_rows = jnp.dot(reorder, reached, precision=lax.Precision.HIGHEST)
    own_cols = jnp.dot(reached_rows, reorder[:half_rows].T, precision=lax.Precision.HIGHEST) > 0.5
    own_depth = jnp.dot(reorder[:half_rows], node_depth, precision=lax.Precision.HIGHEST)
    position = cache_length.astype(jnp.float32) + own_depth
    query_heads = rotate(
        head_norm(queries.astype(jnp.float32).reshape(half_rows, HEADS, HEAD_DIM), query_gain),
        position,
    ).astype(jnp.bfloat16)
    key_heads = rotate(
        head_norm(new_keys.astype(jnp.float32).reshape(half_rows, KV_HEADS, HEAD_DIM), key_gain),
        position,
    ).astype(jnp.bfloat16)
    query_own = query_heads.reshape(half_rows, q_width)
    fresh_own = jnp.concatenate([key_heads.reshape(half_rows, kv_width), new_values], axis=1)
    query_other, fresh_other = swapped((query_own, fresh_own), "tp", 0)
    query_all = jnp.concatenate([query_own, query_other], axis=0)
    limit = (cache_length - pair_side * key_cache.shape[0]).reshape(1)
    run_top, run_total, summed = attend(
        limit,
        query_all,
        key_cache,
        value_cache,
        key_heads.reshape(half_rows, kv_width),
        new_values,
        own_cols.astype(jnp.float32),
    )
    far_top, far_total, far_sum = (
        swapped(run_top[:, :, half_rows:].astype(jnp.bfloat16), "tp", 0).astype(jnp.float32),
        swapped(run_total[:, :, half_rows:].astype(jnp.bfloat16), "tp", 0).astype(jnp.float32),
        swapped(summed[:, :, half_rows:].astype(jnp.bfloat16), "tp", 0).astype(jnp.float32),
    )
    near_top = run_top[:, :, :half_rows]
    joint_top = jnp.maximum(near_top, far_top)
    near_scale = jnp.exp(near_top - joint_top)
    far_scale = jnp.exp(far_top - joint_top)
    denominator = run_total[:, :, :half_rows] * near_scale + far_total * far_scale
    merged = (summed[:, :, :half_rows] * near_scale + far_sum * far_scale) / denominator
    attended = jnp.transpose(merged, (2, 0, 1, 3)).reshape(half_rows, q_width).astype(jnp.bfloat16)
    leaf_pick = (node_ids == leaf_index).astype(jnp.float32)
    leaf_row = jnp.dot(leaf_pick, reached, precision=lax.Precision.HIGHEST)
    out_depths = (pair_side * half_rows + local_ids).astype(jnp.float32)
    chosen = leaf_row[None, :] * (node_depth[None, :] == out_depths[:, None]).astype(jnp.float32)
    chosen = jnp.dot(chosen, reorder.T, precision=lax.Precision.HIGHEST)
    fresh_all = jnp.concatenate([fresh_own, fresh_other], axis=0)
    accepted_kv = jnp.dot(
        chosen.astype(jnp.bfloat16), fresh_all, preferred_element_type=jnp.float32
    ).astype(jnp.bfloat16)
    levels = lax.axis_size("req") // SIDE
    places = SIDE * tp_count
    attn_slice = feature_slices(attended, 0)
    attn_slice, down_sent = lax.optimization_barrier((attn_slice, down_sent))
    down_full = joined(down_kept, swapped(down_sent, "req", 0), 1)
    projected = jnp.dot(attn_slice, out_full, preferred_element_type=jnp.float32)
    projected = projected.astype(jnp.bfloat16).reshape(levels, places, half_rows, -1)
    projected = reduced(projected, "level", "lead", 1).astype(jnp.bfloat16)
    projected = exchange(projected.reshape(places, half_rows, -1), "place", 2)
    own_projected = jnp.transpose(
        projected.reshape(SIDE, tp_count, half_rows, -1), (2, 1, 0, 3)
    ).reshape(half_rows, -1)
    residual = (hidden_in.astype(jnp.float32) + own_projected.astype(jnp.float32)).astype(
        jnp.bfloat16
    )
    residual_wide = residual.astype(jnp.float32)
    mean_sq = jnp.mean(residual_wide * residual_wide, axis=-1, keepdims=True)
    normed = (residual_wide * lax.rsqrt(mean_sq + EPS) * post_gain.astype(jnp.float32)).astype(
        jnp.bfloat16
    )
    normed_slice = feature_slices(normed, 3)
    sums = jnp.dot(normed_slice, gate_up_full, preferred_element_type=jnp.float32)
    sums = sums.astype(jnp.bfloat16).reshape(levels, places, half_rows, -1)
    sums = reduced(sums, "level", "lead", 4).reshape(places * half_rows, -1)
    hidden_width = sums.shape[1] // 2
    hidden = (jax.nn.silu(sums[:, :hidden_width]) * sums[:, hidden_width:]).astype(jnp.bfloat16)
    hidden_all = gathered_levels(hidden, 5).reshape(-1, hidden_width)
    partial_out = jnp.dot(hidden_all, down_full, preferred_element_type=jnp.float32)
    partial_out = partial_out.astype(jnp.bfloat16).reshape(levels, places, half_rows, -1)
    paired_sum = reduced(partial_out, "place", "inner", 6).astype(jnp.bfloat16)
    mlp_own = exchange(paired_sum, "level", 7)
    mlp_own = jnp.transpose(mlp_own, (1, 0, 2)).reshape(half_rows, -1).astype(jnp.float32)
    layer_out = (residual_wide + mlp_own).astype(jnp.bfloat16)
    return (layer_out, accepted_kv)


def solution(mesh):
    in_specs = (
        P(("req", "tp"), None),
        P(("req", "tp"), None),
        P(("req", "tp"), None),
        P(("req", "tp"), None),
        P(("req", "tp"), None),
        P(("req", "tp"), None),
        P(),
        P(),
        P(),
        P(),
        P(),
        P(),
        P("req", "tp"),
        P("req", "tp"),
        P("req", "tp"),
        P("tp", "req"),
    )
    out_specs = (P(("req", "tp"), None), P(("req", "tp"), None))
    return jax.shard_map(
        per_device, mesh=mesh, in_specs=in_specs, out_specs=out_specs, check_vma=False
    )
```

```python
import functools

import jax
import jax.numpy as jnp
from jax import lax
from jax.experimental import pallas as pl
from jax.experimental.pallas import tpu as pltpu
from jax.sharding import PartitionSpec as P

HEADS = 32
KV_HEADS = 8
HEAD_DIM = 128


NEG = -1e30
EPS = 1e-06
ROPE_BASE = 1000000.0


def swapped(value, axis, bit):
    mask = 2**bit
    pairs = [(source, source ^ mask) for source in range(lax.axis_size(axis))]
    return lax.ppermute(value, axis, pairs)


def head_norm(values, gain_vec):
    mean_sq = jnp.mean(values * values, axis=-1, keepdims=True)
    return values * lax.rsqrt(mean_sq + EPS) * gain_vec.astype(jnp.float32)


def rotate(values, position):
    head_width = values.shape[-1]
    half_width = head_width // 2
    frequency = ROPE_BASE ** (-2.0 * jnp.arange(half_width, dtype=jnp.float32) / head_width)
    angles = position[:, None] * frequency[None, :]
    cosine = jnp.cos(angles)[:, None, :]
    sine_part = jnp.sin(angles)[:, None, :]
    front_half = values[..., :half_width]
    back_half = values[..., half_width:]
    return jnp.concatenate(
        [front_half * cosine - back_half * sine_part, back_half * cosine + front_half * sine_part],
        axis=-1,
    )


SIDE = 2
MESH = pl.DeviceIdType.MESH
ANY = pl.BlockSpec(memory_space=pl.ANY)


def meet(peers):
    barrier = pltpu.get_barrier_semaphore()
    for peer in peers:
        pl.semaphore_signal(barrier, inc=1, device_id=peer, device_id_type=MESH)
    pl.semaphore_wait(barrier, len(peers))


def remote(source, target, send_sem, recv_sem, peer):
    return pltpu.make_async_remote_copy(
        src_ref=source,
        dst_ref=target,
        send_sem=send_sem,
        recv_sem=recv_sem,
        device_id=peer,
        device_id_type=MESH,
    )


def line_of(along):
    tp_count = lax.axis_size("tp")
    req, tp = lax.axis_index("req"), lax.axis_index("tp")
    level, side = req // SIDE, req % SIDE
    if along == "level":
        return (
            lax.axis_size("req") // SIDE,
            level,
            lambda index: {"req": index * SIDE + side, "tp": tp},
        )
    return (
        SIDE * tp_count,
        side * tp_count + tp,
        lambda index: {"req": level * SIDE + index // tp_count, "tp": index % tp_count},
    )


def exchange_kernel(along, rows_ref, out_ref, send_sem, recv_sem, own_sem):
    count, mine, device = line_of(along)

    def part(index):
        return rows_ref.at[index]

    others = [(mine + step) % count for step in range(1, count)]
    meet([device(index) for index in others])
    copies = [
        remote(part(index), out_ref.at[mine], send_sem.at[at], recv_sem.at[at], device(index))
        for at, index in enumerate(others)
    ]
    for copy in copies:
        copy.start()
    own = pltpu.make_async_copy(part(mine), out_ref.at[mine], own_sem)
    own.start()
    for copy in copies:
        copy.wait()
    own.wait()


def exchange(rows, along, collective_id):
    count = lax.axis_size("req") // SIDE if along == "level" else SIDE * lax.axis_size("tp")
    part_shape = rows.shape[1:]
    return pl.pallas_call(
        functools.partial(exchange_kernel, along),
        out_shape=jax.ShapeDtypeStruct((count, *part_shape), rows.dtype),
        in_specs=[ANY],
        out_specs=ANY,
        scratch_shapes=[
            pltpu.SemaphoreType.DMA((count - 1,)),
            pltpu.SemaphoreType.DMA((count - 1,)),
            pltpu.SemaphoreType.DMA,
        ],
        compiler_params=pltpu.CompilerParams(collective_id=collective_id, has_side_effects=True),
    )(rows)


def reduce_kernel(
    along, mode, rows_ref, out_ref, landed, held,
    pair_send, pair_recv, far_send, far_recv, last_send, last_recv, own_sems,
):
    count, mine, device = line_of(along)
    half, place, parity = count // 2, mine // 2, mine % 2
    depth = landed.shape[1]
    piece = depth // 2

    def part(index, start, size):
        if mode == "inner":
            return rows_ref.at[pl.ds(start, size), index]
        return rows_ref.at[index, pl.ds(start, size)]

    order = [(place + step) % half for step in range(1, half)]
    pair = device(place * 2 + 1 - parity)
    far_devices = [device(index * 2 + parity) for index in order]
    meet(far_devices + [pair])
    inward, kept, outward = [], [], []
    for at, index in enumerate(order):
        for cut in range(2):
            copy = remote(
                part(index * 2 + 1 - parity, cut * piece, piece),
                landed.at[at, pl.ds(cut * piece, piece)],
                pair_send.at[at * 2 + cut],
                pair_recv.at[at * 2 + cut],
                pair,
            )
            copy.start()
            inward.append(copy)
        copy = pltpu.make_async_copy(
            part(index * 2 + parity, 0, depth), held.at[at], own_sems.at[at + 1]
        )
        copy.start()
        kept.append(copy)
    last = remote(
        part(place * 2 + 1 - parity, 0, depth), out_ref.at[1], last_send, last_recv, pair
    )
    last.start()
    own = pltpu.make_async_copy(part(mine, 0, depth), out_ref.at[0], own_sems.at[0])
    own.start()
    for at, peer in enumerate(far_devices):
        kept[at].wait()
        for cut in range(2):
            inward[at * 2 + cut].wait_recv()

            @pl.loop(cut * piece, (cut + 1) * piece)
            def _(row):
                total = held[at, row].astype(jnp.float32) + landed[at, row].astype(jnp.float32)
                held[at, row] = total.astype(held.dtype)

            copy = remote(
                held.at[at, pl.ds(cut * piece, piece)],
                out_ref.at[at + 2, pl.ds(cut * piece, piece)],
                far_send.at[at * 2 + cut],
                far_recv.at[at * 2 + cut],
                peer,
            )
            copy.start()
            outward.append(copy)
    own.wait()
    last.wait()
    for copy in inward:
        copy.wait_send()
    for copy in outward:
        copy.wait()


def reduced(rows, along, mode, collective_id):
    count = lax.axis_size("req") // SIDE if along == "level" else SIDE * lax.axis_size("tp")
    half = count // 2
    if mode == "inner":
        part_shape = rows.shape[:1] + rows.shape[2:]
    else:
        part_shape = rows.shape[1:]
    parts = pl.pallas_call(
        functools.partial(reduce_kernel, along, mode),
        out_shape=jax.ShapeDtypeStruct((half + 1, *part_shape), rows.dtype),
        in_specs=[ANY],
        out_specs=ANY,
        scratch_shapes=[
            pltpu.VMEM((half - 1, *part_shape), rows.dtype),
            pltpu.VMEM((half - 1, *part_shape), rows.dtype),
            pltpu.SemaphoreType.DMA((2 * (half - 1),)),
            pltpu.SemaphoreType.DMA((2 * (half - 1),)),
            pltpu.SemaphoreType.DMA((2 * (half - 1),)),
            pltpu.SemaphoreType.DMA((2 * (half - 1),)),
            pltpu.SemaphoreType.DMA,
            pltpu.SemaphoreType.DMA,
            pltpu.SemaphoreType.DMA((half,)),
        ],
        compiler_params=pltpu.CompilerParams(
            collective_id=collective_id, has_side_effects=True, vmem_limit_bytes=40 * 2**20
        ),
    )(rows)
    return jnp.sum(parts.astype(jnp.float32), axis=0)


def gather_kernel(rows_ref, out_ref, far_send, far_recv, near_send, near_recv, own_sem):
    count, mine, device = line_of("level")
    half, place, parity = count // 2, mine // 2, mine % 2
    pair = device(place * 2 + 1 - parity)
    order = [(place + step) % half for step in range(1, half)]
    far_devices = [device(index * 2 + parity) for index in order]
    meet(far_devices + [pair])
    far, near = [], []
    for cut in range(2):
        for peer in far_devices:
            at = len(far)
            copy = remote(
                rows_ref.at[cut], out_ref.at[mine, cut], far_send.at[at], far_recv.at[at], peer
            )
            copy.start()
            far.append(copy)
    own = pltpu.make_async_copy(rows_ref, out_ref.at[mine], own_sem)
    own.start()
    for cut in range(2):
        at = len(near)
        copy = remote(
            rows_ref.at[cut], out_ref.at[mine, cut], near_send.at[at], near_recv.at[at], pair
        )
        copy.start()
        near.append(copy)
    for cut in range(2):
        for step in range(1, half):
            far[cut * (half - 1) + step - 1].wait_recv()
            landed = out_ref.at[((place - step + half) % half) * 2 + parity, cut]
            at = len(near)
            copy = remote(landed, landed, near_send.at[at], near_recv.at[at], pair)
            copy.start()
            near.append(copy)
    own.wait()
    for copy in near:
        copy.wait()
    for copy in far:
        copy.wait_send()


def gathered_levels(rows, collective_id):
    count = lax.axis_size("req") // SIDE
    half = count // 2
    rows = rows.reshape(2, rows.shape[0] // 2, rows.shape[1])
    return pl.pallas_call(
        gather_kernel,
        out_shape=jax.ShapeDtypeStruct((count, *rows.shape), rows.dtype),
        in_specs=[ANY],
        out_specs=ANY,
        scratch_shapes=[
            pltpu.SemaphoreType.DMA((2 * (half - 1),)),
            pltpu.SemaphoreType.DMA((2 * (half - 1),)),
            pltpu.SemaphoreType.DMA((2 * half,)),
            pltpu.SemaphoreType.DMA((2 * half,)),
            pltpu.SemaphoreType.DMA,
        ],
        compiler_params=pltpu.CompilerParams(collective_id=collective_id, has_side_effects=True),
    )(rows)


def slices_kernel(
    rows_ref, out_ref, send_level, recv_level, send_far, recv_far, send_core, recv_core, own_sem
):
    tp_count = lax.axis_size("tp")
    levels = lax.axis_size("req") // SIDE
    req, tp = lax.axis_index("req"), lax.axis_index("tp")
    level, side = req // SIDE, req % SIDE
    place = side * tp_count + tp
    core, chip = tp % 2, place // 2
    chips = SIDE * tp_count // 2
    width = rows_ref.shape[1] // levels

    def columns(index):
        return rows_ref.at[:, pl.ds(pl.multiple_of(index * width, width), width)]

    def chip_place(index):
        return index * 2 + core

    def device(at):
        return {"req": level * SIDE + at // tp_count, "tp": at % tp_count}

    level_ids = [(level + step) % levels for step in range(1, levels)]
    level_devices = [{"req": index * SIDE + side, "tp": tp} for index in level_ids]
    far_devices = [device(chip_place((chip + step) % chips)) for step in range(1, chips)]
    core_device = device(chip * 2 + 1 - core)
    meet(level_devices + far_devices + [core_device])
    first = [
        remote(columns(index), out_ref.at[level, place], send_level.at[at], recv_level.at[at], peer)
        for at, (index, peer) in enumerate(zip(level_ids, level_devices))
    ]
    for copy in first:
        copy.start()
    own = pltpu.make_async_copy(columns(level), out_ref.at[level, place], own_sem)
    own.start()
    far, near = [], []
    for step in range(levels):
        source_level = (level - step + levels) % levels
        target = out_ref.at[source_level, place]
        if step > 0:
            first[step - 1].wait_recv()
        source = columns(level) if step == 0 else target
        for peer in far_devices:
            at = len(far)
            copy = remote(source, target, send_far.at[at], recv_far.at[at], peer)
            copy.start()
            far.append(copy)
        at = len(near)
        copy = remote(source, target, send_core.at[at], recv_core.at[at], core_device)
        copy.start()
        near.append(copy)
    for step in range(levels):
        source_level = (level - step + levels) % levels
        for hop in range(1, chips):
            far[step * (chips - 1) + hop - 1].wait_recv()
            landed = out_ref.at[source_level, chip_place((chip - hop + chips) % chips)]
            at = len(near)
            copy = remote(landed, landed, send_core.at[at], recv_core.at[at], core_device)
            copy.start()
            near.append(copy)
    own.wait()
    for copy in near:
        copy.wait()
    for copy in first + far:
        copy.wait_send()


def feature_slices(rows, collective_id):
    levels = lax.axis_size("req") // SIDE
    places = SIDE * lax.axis_size("tp")
    width = rows.shape[1] // levels
    chips = places // 2
    gathered = pl.pallas_call(
        slices_kernel,
        out_shape=jax.ShapeDtypeStruct((levels, places, rows.shape[0], width), rows.dtype),
        in_specs=[ANY],
        out_specs=ANY,
        scratch_shapes=[
            pltpu.SemaphoreType.DMA((levels - 1,)),
            pltpu.SemaphoreType.DMA((levels - 1,)),
            pltpu.SemaphoreType.DMA((levels * (chips - 1),)),
            pltpu.SemaphoreType.DMA((levels * (chips - 1),)),
            pltpu.SemaphoreType.DMA((levels * chips,)),
            pltpu.SemaphoreType.DMA((levels * chips,)),
            pltpu.SemaphoreType.DMA,
        ],
        compiler_params=pltpu.CompilerParams(collective_id=collective_id, has_side_effects=True),
    )(rows)
    return gathered.reshape(-1, width)


def paired_halves(shard, axis):
    side = lax.axis_index("req") % SIDE
    half = shard.shape[axis] // 2
    kept = lax.dynamic_slice_in_dim(shard, side * half, half, axis)
    sent = lax.dynamic_slice_in_dim(shard, (1 - side) * half, half, axis)
    return kept, sent


def joined(kept, received, axis):
    side = lax.axis_index("req") % SIDE
    low = jnp.where(side == 0, kept, received)
    high = jnp.where(side == 0, received, kept)
    return jnp.concatenate([low, high], axis=axis)


def attention_kernel(
    limit_ref, query_ref, key_ref, value_ref, fresh_key_ref, fresh_value_ref, allowed_ref,
    top_ref, total_ref, sum_ref,
):
    group_size = query_ref.shape[1] // HEAD_DIM
    query = jnp.concatenate(
        [query_ref[:, at * HEAD_DIM : (at + 1) * HEAD_DIM] for at in range(group_size)], axis=0
    )
    score_scale = HEAD_DIM ** (-0.5)
    limit = limit_ref[0]
    chunk = key_ref.shape[0] // 4

    def score(keys):
        return (
            lax.dot_general(
                query, keys, (((1,), (1,)), ((), ())), preferred_element_type=jnp.float32
            )
            * score_scale
        )

    def weigh(scores, top, allowed):
        weights = jnp.where(allowed, jnp.exp(scores - top), 0.0).astype(jnp.bfloat16)
        return weights, jnp.sum(weights.astype(jnp.float32), axis=-1, keepdims=True)

    allowed = jnp.concatenate([allowed_ref[...]] * group_size, axis=0) > 0.5
    scores = jnp.where(allowed, score(fresh_key_ref[...]), NEG)
    top = jnp.max(scores, axis=-1, keepdims=True)
    weights, total = weigh(scores, top, allowed)
    summed = jnp.dot(weights, fresh_value_ref[...], preferred_element_type=jnp.float32)

    def step(index, running):
        top, total, summed = running
        start = pl.multiple_of(index * chunk, chunk)
        keys = key_ref[pl.ds(start, chunk), :]
        values = value_ref[pl.ds(start, chunk), :]
        allowed = lax.broadcasted_iota(jnp.int32, (query.shape[0], chunk), 1) + start < limit
        scores = jnp.where(allowed, score(keys), NEG)
        new_top = jnp.maximum(top, jnp.max(scores, axis=-1, keepdims=True))
        weights, chunk_total = weigh(scores, new_top, allowed)
        shrink = jnp.exp(top - new_top)
        summed = summed * shrink + jnp.dot(weights, values, preferred_element_type=jnp.float32)
        return new_top, total * shrink + chunk_total, summed

    live = jnp.clip((limit + chunk - 1) // chunk, 0, 4)
    top, total, summed = lax.fori_loop(0, live, step, (top, total, summed))
    top_ref[0] = top
    total_ref[0] = total
    sum_ref[0] = summed


def attend(limit, query, keys, values, fresh_keys, fresh_values, allowed):
    rows, fresh_rows, cached_rows = query.shape[0], fresh_keys.shape[0], keys.shape[0]
    group_size = HEADS // KV_HEADS
    group_rows = rows * group_size

    def columns(block_rows, width):
        return pl.BlockSpec((block_rows, width), lambda head, limit_ref: (0, head))

    def lead(width):
        return pl.BlockSpec((1, group_rows, width), lambda head, limit_ref: (head, 0, 0))

    results = pl.pallas_call(
        attention_kernel,
        out_shape=[
            jax.ShapeDtypeStruct((KV_HEADS, group_rows, width), jnp.float32)
            for width in (1, 1, HEAD_DIM)
        ],
        grid_spec=pltpu.PrefetchScalarGridSpec(
            num_scalar_prefetch=1,
            grid=(KV_HEADS,),
            in_specs=[
                columns(rows, group_size * HEAD_DIM),
                columns(cached_rows, HEAD_DIM),
                columns(cached_rows, HEAD_DIM),
                columns(fresh_rows, HEAD_DIM),
                columns(fresh_rows, HEAD_DIM),
                pl.BlockSpec((rows, fresh_rows), lambda head, limit_ref: (0, 0)),
            ],
            out_specs=[lead(1), lead(1), lead(HEAD_DIM)],
        ),
        compiler_params=pltpu.CompilerParams(vmem_limit_bytes=32 * 2**20),
        cost_estimate=pl.CostEstimate(
            flops=4 * group_rows * cached_rows * KV_HEADS * HEAD_DIM,
            bytes_accessed=4 * cached_rows * KV_HEADS * HEAD_DIM,
            transcendentals=group_rows * cached_rows * KV_HEADS,
        ),
    )(limit, query, keys, values, fresh_keys, fresh_values, allowed)
    return [
        result.reshape(KV_HEADS, group_size, rows, result.shape[2]) for result in results
    ]


def ancestors(parent_row):
    node_count = parent_row.shape[0]
    node_ids = jnp.arange(node_count, dtype=jnp.int32)
    identity_mat = (node_ids[:, None] == node_ids[None, :]).astype(jnp.float32)
    parent_mat = (parent_row[:, None] == node_ids[None, :]).astype(jnp.float32) * (
        1.0 - identity_mat
    )
    reached = jnp.minimum(identity_mat + parent_mat, 1.0)
    for sweep in range(node_count.bit_length()):
        reached = jnp.minimum(jnp.dot(reached, reached, precision=lax.Precision.HIGHEST), 1.0)
    return reached


def per_device(
    hidden_in,
    queries,
    new_keys,
    new_values,
    key_cache,
    value_cache,
    cache_lengths,
    parent_ids,
    accepted_leaf,
    query_gain,
    key_gain,
    post_gain,
    out_weight,
    gate_weight,
    up_weight,
    down_weight,
):
    half_rows = queries.shape[0]
    out_kept, out_sent = paired_halves(out_weight, 1)
    out_received = swapped(out_sent, "req", 0)
    gate_kept, gate_sent = paired_halves(gate_weight, 1)
    up_kept, up_sent = paired_halves(up_weight, 1)
    gate_up_received = swapped(jnp.concatenate([gate_sent, up_sent], axis=1), "req", 0)
    gate_up_kept = jnp.concatenate([gate_kept, up_kept], axis=1)
    down_kept, down_sent = paired_halves(down_weight, 0)
    out_full = joined(out_kept, out_received, 0)
    gate_up_full = joined(gate_up_kept, gate_up_received, 0)
    tree_size = 2 * half_rows
    kv_width = new_keys.shape[1]
    q_width = queries.shape[1]
    tp_count = lax.axis_size("tp")
    device = lax.axis_index(("req", "tp"))
    request = device // 2
    pair_side = lax.axis_index("tp") % 2
    cache_length = lax.dynamic_index_in_dim(cache_lengths, request, 0, keepdims=False)
    parent_row = lax.dynamic_index_in_dim(parent_ids, request, 0, keepdims=False)
    leaf_index = lax.dynamic_index_in_dim(accepted_leaf, request, 0, keepdims=False)
    reached = ancestors(parent_row)
    node_depth = jnp.sum(reached, axis=1) - 1.0
    node_ids = jnp.arange(tree_size, dtype=jnp.int32)
    local_ids = jnp.arange(half_rows, dtype=jnp.int32)
    node_order = jnp.concatenate(
        [pair_side * half_rows + local_ids, (1 - pair_side) * half_rows + local_ids]
    )
    reorder = (node_order[:, None] == node_ids[None, :]).astype(jnp.float32)
    reached_rows = jnp.dot(reorder, reached, precision=lax.Precision.HIGHEST)
    own_cols = jnp.dot(reached_rows, reorder[:half_rows].T, precision=lax.Precision.HIGHEST) > 0.5
    own_depth = jnp.dot(reorder[:half_rows], node_depth, precision=lax.Precision.HIGHEST)
    position = cache_length.astype(jnp.float32) + own_depth
    query_heads = rotate(
        head_norm(queries.astype(jnp.float32).reshape(half_rows, HEADS, HEAD_DIM), query_gain),
        position,
    ).astype(jnp.bfloat16)
    key_heads = rotate(
        head_norm(new_keys.astype(jnp.float32).reshape(half_rows, KV_HEADS, HEAD_DIM), key_gain),
        position,
    ).astype(jnp.bfloat16)
    query_own = query_heads.reshape(half_rows, q_width)
    fresh_own = jnp.concatenate([key_heads.reshape(half_rows, kv_width), new_values], axis=1)
    query_other, fresh_other = swapped((query_own, fresh_own), "tp", 0)
    query_all = jnp.concatenate([query_own, query_other], axis=0)
    limit = (cache_length - pair_side * key_cache.shape[0]).reshape(1)
    run_top, run_total, summed = attend(
        limit,
        query_all,
        key_cache,
        value_cache,
        key_heads.reshape(half_rows, kv_width),
        new_values,
        own_cols.astype(jnp.float32),
    )
    far_top, far_total, far_sum = (
        swapped(run_top[:, :, half_rows:].astype(jnp.bfloat16), "tp", 0).astype(jnp.float32),
        swapped(run_total[:, :, half_rows:].astype(jnp.bfloat16), "tp", 0).astype(jnp.float32),
        swapped(summed[:, :, half_rows:].astype(jnp.bfloat16), "tp", 0).astype(jnp.float32),
    )
    near_top = run_top[:, :, :half_rows]
    joint_top = jnp.maximum(near_top, far_top)
    near_scale = jnp.exp(near_top - joint_top)
    far_scale = jnp.exp(far_top - joint_top)
    denominator = run_total[:, :, :half_rows] * near_scale + far_total * far_scale
    merged = (summed[:, :, :half_rows] * near_scale + far_sum * far_scale) / denominator
    attended = jnp.transpose(merged, (2, 0, 1, 3)).reshape(half_rows, q_width).astype(jnp.bfloat16)
    leaf_pick = (node_ids == leaf_index).astype(jnp.float32)
    leaf_row = jnp.dot(leaf_pick, reached, precision=lax.Precision.HIGHEST)
    out_depths = (pair_side * half_rows + local_ids).astype(jnp.float32)
    chosen = leaf_row[None, :] * (node_depth[None, :] == out_depths[:, None]).astype(jnp.float32)
    chosen = jnp.dot(chosen, reorder.T, precision=lax.Precision.HIGHEST)
    fresh_all = jnp.concatenate([fresh_own, fresh_other], axis=0)
    accepted_kv = jnp.dot(
        chosen.astype(jnp.bfloat16), fresh_all, preferred_element_type=jnp.float32
    ).astype(jnp.bfloat16)
    levels = lax.axis_size("req") // SIDE
    places = SIDE * tp_count
    attn_slice = feature_slices(attended, 0)
    projected = jnp.dot(attn_slice, out_full, preferred_element_type=jnp.float32)
    projected = projected.astype(jnp.bfloat16).reshape(levels, places, half_rows, -1)
    projected = reduced(projected, "level", "lead", 1).astype(jnp.bfloat16)
    projected = exchange(projected.reshape(places, half_rows, -1), "place", 2)
    own_projected = jnp.transpose(
        projected.reshape(SIDE, tp_count, half_rows, -1), (2, 1, 0, 3)
    ).reshape(half_rows, -1)
    residual = (hidden_in.astype(jnp.float32) + own_projected.astype(jnp.float32)).astype(
        jnp.bfloat16
    )
    residual_wide = residual.astype(jnp.float32)
    mean_sq = jnp.mean(residual_wide * residual_wide, axis=-1, keepdims=True)
    normed = (residual_wide * lax.rsqrt(mean_sq + EPS) * post_gain.astype(jnp.float32)).astype(
        jnp.bfloat16
    )
    normed_slice = feature_slices(normed, 3)
    normed_slice, down_sent = lax.optimization_barrier((normed_slice, down_sent))
    down_full = joined(down_kept, swapped(down_sent, "req", 0), 1)
    sums = jnp.dot(normed_slice, gate_up_full, preferred_element_type=jnp.float32)
    sums = sums.astype(jnp.bfloat16).reshape(levels, places, half_rows, -1)
    sums = reduced(sums, "level", "lead", 4).reshape(places * half_rows, -1)
    hidden_width = sums.shape[1] // 2
    hidden = (jax.nn.silu(sums[:, :hidden_width]) * sums[:, hidden_width:]).astype(jnp.bfloat16)
    hidden_all = gathered_levels(hidden, 5).reshape(-1, hidden_width)
    partial_out = jnp.dot(hidden_all, down_full, preferred_element_type=jnp.float32)
    partial_out = partial_out.astype(jnp.bfloat16).reshape(levels, places, half_rows, -1)
    paired_sum = reduced(partial_out, "place", "inner", 6).astype(jnp.bfloat16)
    mlp_own = exchange(paired_sum, "level", 7)
    mlp_own = jnp.transpose(mlp_own, (1, 0, 2)).reshape(half_rows, -1).astype(jnp.float32)
    layer_out = (residual_wide + mlp_own).astype(jnp.bfloat16)
    return (layer_out, accepted_kv)


def solution(mesh):
    in_specs = (
        P(("req", "tp"), None),
        P(("req", "tp"), None),
        P(("req", "tp"), None),
        P(("req", "tp"), None),
        P(("req", "tp"), None),
        P(("req", "tp"), None),
        P(),
        P(),
        P(),
        P(),
        P(),
        P(),
        P("req", "tp"),
        P("req", "tp"),
        P("req", "tp"),
        P("tp", "req"),
    )
    out_specs = (P(("req", "tp"), None), P(("req", "tp"), None))
    return jax.shard_map(
        per_device, mesh=mesh, in_specs=in_specs, out_specs=out_specs, check_vma=False
    )
```
